256 devices in a mesh: vir: 32 (over z, y), fit: 8 (over x, core).
Axes of the slice: x: 4, y: 4, z: 8, core: 2. Of those that a mesh axis runs over, the one named last changes fastest.
Arguments:
- fitted: bfloat16 [2, 2400, 24, 7168], P(None, 'vir', None, 'fit'), may hold values from -0.0234375 to 0.0234375
- vcouple: bfloat16 [2, 2400, 2400], P(None, 'fit'), may hold values from -0.125 to 0.125
- actfock: float32 [2, 24, 24], replicated, may hold values from -1.25 to 1.25
- eps_vir: float32 [2400], P('vir'), may hold values from 0.5 to 4
- eps_act: float32 [24], replicated, may hold values from -0.5 to 0.5
- pair_energy: float32 [64], replicated, may hold values from -3 to -2
- source: float32 [2, 2400, 1536], P(None, 'vir'), may hold values from -6 to 6
Outputs:
- amplitude: float32 [2, 2400, 1536], P(None, 'vir')
The draws below stay inside these ranges and needn't reach their ends.
All inputs are finite; a program needn't handle non-finite values.
Results may differ from the reference program's by a relative error of at most 0.0026.
Values may be sent and summed in bfloat16 or wider, within the bound.
No kernel may reach another device: no remote copies, remote signals or barrier semaphores. Data moves between devices by JAX's collectives and lax.ppermute only.
A program may use at most 128 MiB of HBM per device.

```python
import math
import jax
import jax.numpy as jnp
from jax import lax

NACT = 24
NVIR = 2400
NFIT = 7168
PAIRS = 64
PASSES = 3


def steps_of(rng, shape, split, low, top_value):
    factor_of = 1.0
    for position, blocks in split:
        draws = jax.random.uniform(jax.random.fold_in(jax.random.fold_in(rng, 6), position), (blocks,), jnp.float32, low / len(split), top_value / len(split))
        factor_of = factor_of * jnp.repeat(jnp.exp(draws), shape[position] // blocks).reshape((-1,) + (1,) * (len(shape) - 1 - position))
    return factor_of


def scatter_about(rng, shape, scale, bound, shards=(), kind=jnp.bfloat16):
    entries = scale * jax.random.normal(rng, shape, jnp.float32)
    if shards:
        entries = entries * steps_of(rng, shape, shards, -0.22, 0.18)
    return jnp.clip(entries, -bound, bound).astype(kind)


def setup_inputs(seed: int = 0) -> dict:
    arg_keys = jax.random.split(jax.random.key(seed), 8)
    fitted = scatter_about(arg_keys[0], (2, NVIR, NACT, NFIT), (NACT * NVIR) ** -0.5, 0.0234375, ((1, 32), (3, 8)))
    vcouple = scatter_about(arg_keys[1], (2, NVIR, NVIR), NVIR ** -0.5, 0.125, ((1, 8),))
    actfock = scatter_about(arg_keys[2], (2, NACT, NACT), NACT ** -0.5, 1.25, (), jnp.float32)
    eps_vir = jnp.clip(jnp.exp(math.log(4.0) - 2.0794415 * jax.random.uniform(arg_keys[3], (NVIR,), jnp.float32) ** steps_of(arg_keys[3], (NVIR,), ((0, 32),), -0.2, 0.2)), 0.5, 4.0)
    eps_act = jnp.clip(jax.random.uniform(arg_keys[4], (NACT,), jnp.float32, -0.5, 0.5), -0.5, 0.5)
    pair_energy = jnp.clip(jax.random.uniform(arg_keys[5], (PAIRS,), jnp.float32, -3.0, -2.0), -3.0, -2.0)
    source = scatter_about(arg_keys[6], (2, NVIR, NACT * PAIRS), 1.0, 6.0, ((1, 32),), jnp.float32)
    return {"fitted": fitted, "vcouple": vcouple, "actfock": actfock, "eps_vir": eps_vir, "eps_act": eps_act, "pair_energy": pair_energy, "source": source}


def product(left, right):
    return jnp.dot(left, right, precision=lax.Precision.HIGHEST, preferred_element_type=jnp.float32)


def product_first(left, right):
    return lax.dot_general(left, right, (((0,), (0,)), ((), ())), precision=lax.Precision.HIGHEST, preferred_element_type=jnp.float32)


def reference(fitted, vcouple, actfock, eps_vir, eps_act, pair_energy, source):
    highest = lax.Precision.HIGHEST
    denominator = (eps_vir[:, None, None] + eps_act[None, :, None] - pair_energy[None, None, :]).reshape(NVIR, NACT * PAIRS)
    amplitude = source / denominator[None]
    width = NVIR * NACT
    fit_block = NFIT // 8
    fit_real = fitted[0].reshape(width, NFIT)
    fit_imag = fitted[1].reshape(width, NFIT)
    couple_real = vcouple[0].astype(jnp.float32)
    couple_imag = vcouple[1].astype(jnp.float32)
    for pass_index in range(PASSES):
        rounded = amplitude.astype(jnp.bfloat16)
        flat_real = rounded[0].reshape(width, PAIRS).astype(jnp.float32)
        flat_imag = rounded[1].reshape(width, PAIRS).astype(jnp.float32)

        def block(carry, index):
            start = (index * fit_block).astype(jnp.int32)
            piece_real = lax.dynamic_slice_in_dim(fit_real, start, fit_block, 1).astype(jnp.float32)
            piece_imag = lax.dynamic_slice_in_dim(fit_imag, start, fit_block, 1).astype(jnp.float32)
            over_real = product_first(piece_real, flat_real) + product_first(piece_imag, flat_imag)
            over_imag = product_first(piece_real, flat_imag) - product_first(piece_imag, flat_real)
            over_real = lax.optimization_barrier(over_real.astype(jnp.bfloat16)).astype(jnp.float32)
            over_imag = lax.optimization_barrier(over_imag.astype(jnp.bfloat16)).astype(jnp.float32)
            sum_real = carry[0] + product(piece_real, over_real) - product(piece_imag, over_imag)
            sum_imag = carry[1] + product(piece_real, over_imag) + product(piece_imag, over_real)
            return (sum_real, sum_imag), None

        zeros = jnp.zeros((width, PAIRS), jnp.float32)
        sums, ignored = lax.scan(block, (zeros, zeros), jnp.arange(8, dtype=jnp.int32))
        fitted_term = jnp.stack([sums[0], sums[1]]).reshape(2, NVIR, NACT * PAIRS)
        rows_real = rounded[0].astype(jnp.float32)
        rows_imag = rounded[1].astype(jnp.float32)
        vir_real = product_first(couple_real, rows_real) - product_first(couple_imag, rows_imag)
        vir_imag = product_first(couple_imag, rows_real) + product_first(couple_real, rows_imag)
        virtual_term = jnp.stack([vir_real, vir_imag])
        values = amplitude.reshape(2, NVIR, NACT, PAIRS)
        act_real = jnp.einsum("aup,ut->atp", values[0], actfock[0], precision=highest) - jnp.einsum("aup,ut->atp", values[1], actfock[1], precision=highest)
        act_imag = jnp.einsum("aup,ut->atp", values[0], actfock[1], precision=highest) + jnp.einsum("aup,ut->atp", values[1], actfock[0], precision=highest)
        active_term = jnp.stack([act_real, act_imag]).reshape(2, NVIR, NACT * PAIRS)
        residual = source - denominator[None] * amplitude - active_term - fitted_term - virtual_term
        amplitude = amplitude + residual / denominator[None]
    return amplitude
```

```python
import jax
import jax.numpy as jnp
from jax import lax
from jax.sharding import Mesh
from jax.sharding import PartitionSpec as P

PASSES = 3
VIR = ("z", "y")
FIT = ("x", "c")
F32 = jnp.float32
BF16 = jnp.bfloat16


def to_all(block, axis):
    copies = jnp.broadcast_to(block[None], (lax.axis_size(axis), *block.shape))
    return lax.all_to_all(copies, axis, 0, 0, tiled=True)


def turned(both):
    half = both.shape[-1] // 2
    return jnp.concatenate([-both[..., half:], both[..., :half]], axis=-1)


def dot(left, right, dims):
    return lax.dot_general(left, right, (dims, ((), ())), preferred_element_type=F32)


def halves(values, core, half):
    mine = lax.dynamic_slice_in_dim(values, core * half, half, 3)
    return jnp.concatenate([mine[0], mine[1]], axis=-1)


def per_device(fitted, vcouple, actfock, eps_vir, eps_act, pair_energy, source):
    cores, nx, ny, nz = (lax.axis_size(n) for n in ("c", "x", "y", "z"))
    vir_count = ny * nz
    core = lax.axis_index("c")
    _, avir, act, nfit = fitted.shape
    pairs = pair_energy.shape[0]
    half = pairs // cores
    width = avir * act
    swap = [(0, 1), (1, 0)]
    other = lax.ppermute(fitted, "c", swap)
    mats = [m.reshape(width, nfit) for m in (fitted[0], fitted[1], other[0], other[1])]

    mine_b = lax.dynamic_slice_in_dim(vcouple, lax.axis_index("y") * avir, avir, 1)
    mine_b = lax.dynamic_slice_in_dim(mine_b, lax.axis_index("z") * avir * ny, avir * ny, 2)
    couple = to_all(mine_b, FIT)
    couple_re = couple[:, 0].reshape(nz * avir, ny * avir)
    couple_im = couple[:, 1].reshape(nz * avir, ny * avir)

    energy = lax.dynamic_slice_in_dim(pair_energy, core * half, half, 0)
    energy = jnp.concatenate([energy, energy])
    denom = eps_vir[:, None, None] + eps_act[None, :, None] - energy[None, None, :]
    start = halves(source.reshape(2, avir, act, pairs), core, half) / denom
    amplitude = start
    share = act // nx
    first_act = lax.axis_index("x") * share
    for _ in range(PASSES):
        rounded = amplitude.astype(BF16)
        turn = turned(rounded)
        flat, flat_turn = rounded.reshape(width, 2 * half), turn.reshape(width, 2 * half)
        first = ((0,), (0,))
        part = jnp.concatenate(
            [
                dot(mats[2 * i], flat, first) - dot(mats[2 * i + 1], flat_turn, first)
                for i in range(2)
            ],
            axis=1,
        )
        part = part.astype(BF16).reshape(vir_count, nfit // vir_count, 4 * half)
        part = lax.all_to_all(part, VIR, 0, 0, tiled=True)
        inter = jnp.sum(part.astype(F32), axis=0).astype(BF16)

        block = lax.dynamic_slice_in_dim(rounded, first_act, share, 1)
        block = to_all(block.reshape(avir, share * 2 * half), "z")
        block = block.reshape(nz * avir, share, 2 * half)
        vir = dot(couple_re, block, first) + dot(couple_im, turned(block), first)
        vir = lax.all_to_all(
            vir.astype(BF16).reshape(ny, avir, share * 2 * half), "y", 0, 0, tiled=True
        )
        vir = jnp.sum(vir.astype(F32), axis=0).reshape(avir, share, 2 * half)

        inter = to_all(inter, VIR).reshape(nfit, 4 * half)
        total = jnp.zeros((width, 2 * half), F32)
        for i in range(2):
            here = inter[:, i * 2 * half : (i + 1) * 2 * half]
            total += dot(mats[2 * i], here, ((1,), (0,)))
            total += dot(mats[2 * i + 1], turned(here), ((1,), (0,)))
        total = total.reshape(avir, act, 2 * half)
        old = lax.dynamic_slice_in_dim(total, first_act, share, 1)
        total = lax.dynamic_update_slice_in_dim(total, old + vir, first_act, 1)
        send = total.astype(BF16).reshape(avir * act // 2, 4 * half)
        total = jnp.sum(to_all(send, "x").astype(F32), axis=0).reshape(avir, act, 2 * half)

        highest = lax.Precision.HIGHEST
        active = jnp.einsum("aup,ut->atp", amplitude, actfock[0], precision=highest)
        active += jnp.einsum("aup,ut->atp", turned(amplitude), actfock[1], precision=highest)
        amplitude = start - (total + active) / denom
    theirs = lax.ppermute(amplitude, "c", swap)
    low = jnp.where(core == 0, amplitude, theirs)
    high = jnp.where(core == 0, theirs, amplitude)
    parts = [
        jnp.concatenate([low[..., s], high[..., s]], axis=-1)
        for s in (slice(0, half), slice(half, 2 * half))
    ]
    return jnp.stack(parts).reshape(2, avir, act * pairs)


def split_mesh(mesh, sizes):
    return Mesh(mesh.devices.reshape(*sizes), ("z", "y", "x", "c"))


def solution(mesh, sizes=(8, 4, 4, 2)):
    in_specs = (
        P(None, VIR, None, FIT),
        P(None, FIT, None),
        P(),
        P(VIR),
        P(),
        P(),
        P(None, VIR, None),
    )
    return jax.shard_map(
        per_device,
        mesh=split_mesh(mesh, sizes),
        in_specs=in_specs,
        out_specs=P(None, VIR, None),
        check_vma=False,
    )
```

```python
import functools

import jax
import jax.numpy as jnp
from jax import lax
from jax.experimental import pallas as pl
from jax.experimental.pallas import tpu as pltpu
from jax.sharding import Mesh
from jax.sharding import PartitionSpec as P

PASSES = 3
VIR = ("z", "y")
FIT = ("x", "c")
F32 = jnp.float32
BF16 = jnp.bfloat16
LANES = 128
GROUP = 10
CHUNK = 512
VMEM_LIMIT = 60 << 20


def low_count(avir):
    return -(-avir // (2 * GROUP)) * GROUP


def lane(shape):
    return lax.broadcasted_iota(jnp.int32, shape, len(shape) - 1)


def turned(both):
    ahead = pltpu.roll(both, LANES - 32, 1)
    behind = pltpu.roll(both, 32, 1)
    return jnp.where((lane(both.shape) & 32) == 0, -ahead, behind)


def merged(left, right):
    first = lane(left.shape) < 64
    return (
        jnp.where(first, left, pltpu.roll(right, 64, 1)),
        jnp.where(first, pltpu.roll(left, 64, 1), right),
    )


def mxu(left, right, dims=((1,), (0,))):
    return lax.dot_general(left, right, (dims, ((), ())), preferred_element_type=F32)


def chunks(rows, width):
    out = []
    for half in range(2):
        end = rows if half == 0 else width - rows
        for at in range(0, end, CHUNK):
            out.append((half, at, min(at + CHUNK, end), half * rows + at))
    return out


def fetches(own, other, buf, sems, parts):
    copies = []
    for n, (_, at, end, row) in enumerate(parts):
        both = []
        for s, ref in enumerate((own, other)):
            where = pl.ds(row, end - at)
            both.append(
                pltpu.make_async_copy(
                    ref.at[:, where, :], buf.at[s, :, where, :], sems.at[n, s]
                )
            )
        copies.append(both)
    for both in copies:
        for copy in both:
            copy.start()
    return copies


def tiles_per_row(nfit, vir_count):
    count = -(-nfit // LANES)
    while 16 * count % (2 * vir_count):
        count += 1
    return count


def active_term(prev_ref, kron, rows, act):
    block = GROUP * act
    parts = []
    for at in range(0, rows, block):
        value = prev_ref[at : at + block, :]
        head = value.astype(BF16)
        tail = (value - head.astype(F32)).astype(BF16)
        both = mxu(kron, jnp.concatenate([head, tail, head], axis=0))
        parts.append(both[:block] + turned(both[block:]))
    return jnp.concatenate(parts, axis=0)


def updated(recv_ref, prev_ref, kron_ref, start_ref, inv_ref, act):
    rows = start_ref.shape[0]
    total = active_term(prev_ref, kron_ref[...], rows, act)
    for i in range(recv_ref.shape[0]):
        total += recv_ref[i].astype(F32)
    return start_ref[...] - total * inv_ref[...]


def head_body(state_ref, part_ref, share_ref, buf, copies, parts, act):
    value = state_ref[...]
    low = state_ref.shape[0] // act
    count = share_ref.shape[0] // low
    first = lax.axis_index("x") * count
    for i in range(0, count, 2):
        both = [state_ref[pl.ds(first + i + k, low, stride=act), :] for k in range(2)]
        share_ref[i * low : (i + 2) * low, :] = jnp.concatenate(both, axis=0).astype(BF16)
    across = value.T
    flips = []
    plain = []
    for half in range(2):
        re = across[64 * half : 64 * half + 32]
        im = across[64 * half + 32 : 64 * half + 64]
        plain.append(jnp.concatenate([re, im], axis=0).astype(BF16))
        flips.append(jnp.concatenate([im, -re], axis=0).astype(BF16))
    sums = [None, None]
    for n, (half, at, end, row) in enumerate(parts):
        for s in range(2):
            copies[n][s].wait()
            here = mxu(plain[half][:, at:end], buf[s, 0, row : row + end - at, :])
            here += mxu(flips[half][:, at:end], buf[s, 1, row : row + end - at, :])
            sums[s] = here if sums[s] is None else sums[s] + here
    nfit = sums[0].shape[1]
    pieces, depth, _ = part_ref.shape
    wide = pieces * depth // LANES
    def tile(slot):
        group, k = divmod(slot, wide)
        if k * LANES >= nfit:
            return jnp.zeros((8, LANES), F32)
        s, at = divmod(group * 8, 64)
        return sums[s][at : at + 8, k * LANES : (k + 1) * LANES]

    for slot in range(0, 16 * wide, 2):
        both = jnp.concatenate([tile(slot), tile(slot + 1)], axis=0).astype(BF16)
        piece, at = divmod(slot * 8, depth)
        part_ref[piece, at : at + 16, :] = both


def prepare(source_ref, vir_ref, act_ref, pair_ref, start_ref, inv_ref, act):
    core = lax.axis_index("c")
    avir = source_ref.shape[1]
    low = start_ref.shape[0] // act
    spare = 2 * low - avir
    at = lane((low, LANES))
    row = lax.broadcasted_iota(jnp.int32, (low, LANES), 0)
    held = (at < 64) | (row < low - spare)

    def lifted(values, fill):
        rest = jnp.full((spare, values.shape[1]), fill, F32)
        return values[:low], jnp.concatenate([values[low:], rest], axis=0)

    above = lifted(jnp.broadcast_to(vir_ref[...], (avir, LANES)), 1.0)
    above = jnp.where(at < 64, above[0], above[1]) - pair_ref[...]
    for pair in range(act // 2):
        sides = []
        for part in range(2):
            values = source_ref[part, :, pair * LANES : (pair + 1) * LANES]
            values = jnp.where(core == 0, values, pltpu.roll(values, LANES - 32, 1))
            sides += lifted(values, 0.0)
        order = (sides[0], sides[2], sides[1], sides[3])
        for k in range(2):
            t = 2 * pair + k
            value = None
            for n in (3, 2, 1, 0):
                shift = (32 * n - 64 * k) % LANES
                moved = pltpu.roll(order[n], shift, 1) if shift else order[n]
                value = moved if value is None else jnp.where(at < 32 * (n + 1), moved, value)
            inverse = jnp.where(held, 1.0 / (above + act_ref[t]), 0.0)
            inv_ref[pl.ds(t, low, stride=act), :] = inverse
            start_ref[pl.ds(t, low, stride=act), :] = value * inverse


def first_kernel(
    act, source_ref, vir_ref, act_ref, pair_ref, own, other,
    start_ref, inv_ref, part_ref, share_ref, buf, sems,
):
    parts = chunks(start_ref.shape[0], own.shape[1])
    copies = fetches(own, other, buf, sems, parts)
    prepare(source_ref, vir_ref, act_ref, pair_ref, start_ref, inv_ref, act)
    head_body(start_ref, part_ref, share_ref, buf, copies, parts, act)


def next_kernel(
    act, recv_ref, prev_ref, kron_ref, start_ref, inv_ref, own, other,
    state_ref, part_ref, share_ref, buf, sems,
):
    parts = chunks(start_ref.shape[0], own.shape[1])
    copies = fetches(own, other, buf, sems, parts)
    state_ref[...] = updated(recv_ref, prev_ref, kron_ref, start_ref, inv_ref, act)
    head_body(state_ref, part_ref, share_ref, buf, copies, parts, act)


def last_kernel(act, recv_ref, prev_ref, kron_ref, start_ref, inv_ref, state_ref):
    state_ref[...] = updated(recv_ref, prev_ref, kron_ref, start_ref, inv_ref, act)


def output_kernel(act, mine_ref, theirs_ref, out_ref):
    core = lax.axis_index("c")
    avir = out_ref.shape[1]
    low = mine_ref.shape[0] // act
    at = lane((low, LANES))
    for pair in range(act // 2):
        order = []
        for k in range(2):
            where = pl.ds(2 * pair + k, low, stride=act)
            mine, theirs = mine_ref[where, :], theirs_ref[where, :]
            order.append(jnp.where(core == 0, mine, theirs))
            order.append(jnp.where(core == 0, theirs, mine))
        for side in range(2):
            for part in range(2):
                value = None
                for n in (3, 2, 1, 0):
                    shift = (32 * n - 64 * side - 32 * part) % LANES
                    moved = pltpu.roll(order[n], shift, 1) if shift else order[n]
                    value = moved if value is None else jnp.where(at < 32 * (n + 1), moved, value)
                rows = low if side == 0 else avir - low
                out_ref[part, pl.ds(side * low, rows), pair * LANES : (pair + 1) * LANES] = value[
                    :rows
                ]


def total_of(ref, at, rows):
    total = ref[0, at : at + rows, :].astype(F32)
    for i in range(1, ref.shape[0]):
        total += ref[i, at : at + rows, :].astype(F32)
    return total


def along_z_kernel(recv_ref, share_ref, out_ref):
    nz, rows, _ = out_ref.shape
    depth = rows - share_ref.shape[0]
    share = share_ref[...]
    for z in range(nz):
        out_ref[z, :depth, :] = total_of(recv_ref, z * depth, depth).astype(BF16)
        out_ref[z, depth:, :] = share


def sum_kernel(recv_ref, out_ref):
    total = total_of(recv_ref, 0, out_ref.shape[1]).astype(BF16)
    for i in range(out_ref.shape[0]):
        out_ref[i] = total


def couple_kernel(recv_ref, couple_ref, out_ref):
    nz, height, _ = recv_ref.shape
    ny, rows, _ = out_ref.shape
    low = couple_ref.shape[1] // (2 * nz)
    base = height - rows
    couple = couple_ref[...]
    half = couple.shape[0] // 2
    for at in range(0, rows, 2 * low):
        lines = []
        for z in range(nz):
            both = recv_ref[z, base + at : base + at + 2 * low, :].astype(F32)
            lines += merged(both[:low], both[low:])
        both = mxu(couple, jnp.concatenate(lines, axis=0).astype(BF16))
        term = both[:half] + turned(both[half:])
        for y in range(ny):
            top = y * 2 * low
            pieces = merged(term[top : top + low], term[top + low : top + 2 * low])
            out_ref[y, at : at + 2 * low, :] = jnp.concatenate(pieces, axis=0).astype(BF16)


def along_y_kernel(inter_ref, vir_ref, out_ref):
    nz, depth, _ = inter_ref.shape
    for y in range(out_ref.shape[0]):
        for z in range(nz):
            out_ref[y, z * depth : (z + 1) * depth, :] = inter_ref[z]
        out_ref[y, nz * depth :, :] = vir_ref[y]


def tail_kernel(act, height, inter_ref, own, other, out_ref, total, buf, sems):
    rows = total.shape[0]
    nfit = own.shape[2]
    parts = chunks(rows, own.shape[1])
    copies = fetches(own, other, buf, sems, parts)
    wide = inter_ref.shape[0] * height // LANES
    tiles = {}
    for slot in range(0, 16 * wide, 2):
        piece, at = divmod(slot * 8, height)
        both = inter_ref[piece, at : at + 16, :].astype(F32)
        tiles[slot], tiles[slot + 1] = both[:8], both[8:]
    count = -(-nfit // LANES)
    lines = [
        jnp.concatenate([tiles[g * wide + k] for k in range(count)], axis=1)
        for g in range(16)
    ]
    zero = jnp.zeros((64, nfit), F32)
    right = []
    for s in range(2):
        re = jnp.concatenate(lines[8 * s : 8 * s + 4], axis=0)
        im = jnp.concatenate(lines[8 * s + 4 : 8 * s + 8], axis=0)
        plain = jnp.concatenate([re, im], axis=0)
        turn = jnp.concatenate([-im, re], axis=0)
        right.append(
            [
                [jnp.concatenate(order, axis=0).astype(BF16) for order in ((v, zero), (zero, v))]
                for v in (plain, turn)
            ]
        )
    last = ((1,), (1,))
    for n, (half, at, end, row) in enumerate(parts):
        here = None
        for s in range(2):
            copies[n][s].wait()
            for k in range(2):
                term = mxu(buf[s, k, row : row + end - at, :], right[s][k][half], last)
                here = term if here is None else here + term
        if half:
            total[at:end, :] += here
        else:
            total[at:end, :] = here
    low = rows // act
    share = (inter_ref.shape[1] - height) // low
    first = lax.axis_index("x") * share
    for i in range(0, share, 2):
        both = total_of(inter_ref, height + i * low, 2 * low)
        for k in range(2):
            where = pl.ds(first + i + k, low, stride=act)
            total[where, :] = total[where, :] + both[k * low : (k + 1) * low]
    value = total[...].astype(BF16)
    for i in range(out_ref.shape[0]):
        out_ref[i] = value


VMEM = pl.BlockSpec(memory_space=pltpu.VMEM)
HBM = pl.BlockSpec(memory_space=pltpu.HBM)
SMEM = pl.BlockSpec(memory_space=pltpu.SMEM)


def call(body, outs, ins, scratch=(), name=None, flops=0, moved=0):
    return pl.pallas_call(
        body,
        out_shape=outs,
        in_specs=ins,
        out_specs=jax.tree.map(lambda _: VMEM, outs),
        scratch_shapes=scratch,
        compiler_params=pltpu.CompilerParams(vmem_limit_bytes=VMEM_LIMIT),
        cost_estimate=pl.CostEstimate(flops=flops, bytes_accessed=moved, transcendentals=0),
        name=name,
    )


def exchange(copies, axis):
    return lax.all_to_all(copies, axis, 0, 0, tiled=True)


def per_device(fitted, vcouple, actfock, eps_vir, eps_act, pair_energy, source):
    cores, nx, ny, nz = (lax.axis_size(n) for n in ("c", "x", "y", "z"))
    core = lax.axis_index("c")
    _, avir, act, nfit = fitted.shape
    pairs = pair_energy.shape[0]
    half = pairs // cores
    width = avir * act
    low = low_count(avir)
    rows = low * act
    share = act // nx
    swap = [(0, 1), (1, 0)]
    own = fitted.reshape(2, width, nfit)
    other = lax.ppermute(own, "c", swap)

    mine = lax.dynamic_slice_in_dim(vcouple, lax.axis_index("y") * avir, avir, 1)
    mine = lax.dynamic_slice_in_dim(mine, lax.axis_index("z") * avir * ny, avir * ny, 2)
    couple = exchange(jnp.broadcast_to(mine[None], (nz, *mine.shape)), FIT)
    couple = couple.reshape(nz, 2, avir, ny, avir)
    fill = (0, 2 * low - avir)
    couple = jnp.pad(couple, ((0, 0), (0, 0), fill, (0, 0), fill))
    couple = couple.transpose(1, 3, 4, 0, 2).reshape(2 * ny * 2 * low, nz * 2 * low)

    block = GROUP * act
    kron = jnp.concatenate([jnp.kron(jnp.eye(GROUP, dtype=F32), actfock[i].T) for i in range(2)])
    head = kron.astype(BF16)
    rest = (kron - head.astype(F32)).astype(BF16)
    kron = jnp.concatenate([head, head, rest], axis=1)

    energy = lax.dynamic_slice_in_dim(pair_energy, core * half, half, 0)
    energy = jnp.tile(energy, LANES // half).reshape(1, LANES)

    wide = tiles_per_row(nfit, ny * nz)
    height = 16 * wide * 8 // ny
    depth = height // nz
    extra = share * low

    def sent(*shape):
        return jax.ShapeDtypeStruct((*shape, LANES), BF16)

    state_shape = jax.ShapeDtypeStruct((rows, LANES), F32)
    part_shape, share_shape = sent(ny, height), sent(extra)
    steps = len(chunks(rows, width))
    fetch = [pltpu.VMEM((2, 2, width, nfit), BF16), pltpu.SemaphoreType.DMA((steps, 2))]
    flops = 16 * width * nfit * 32
    moved = 8 * width * nfit
    first = call(
        functools.partial(first_kernel, act),
        (state_shape, state_shape, part_shape, share_shape),
        [VMEM, VMEM, SMEM, VMEM, HBM, HBM], fetch, "first", flops, moved,
    )
    later = call(
        functools.partial(next_kernel, act), (state_shape, part_shape, share_shape),
        [VMEM] * 5 + [HBM] * 2, fetch, "later", flops, moved,
    )
    last = call(functools.partial(last_kernel, act), state_shape, [VMEM] * 5, (), "last")
    along_z = call(along_z_kernel, sent(nz, depth + extra), [VMEM] * 2, (), "along_z")
    summed = call(sum_kernel, sent(nz, depth), [VMEM], (), "summed")
    coupled = call(couple_kernel, sent(ny, extra), [VMEM] * 2, (), "coupled")
    along_y = call(along_y_kernel, sent(ny, height + extra), [VMEM] * 2, (), "along_y")
    tail = call(
        functools.partial(tail_kernel, act, height), sent(nx, rows), [VMEM, HBM, HBM],
        [pltpu.VMEM((rows, LANES), F32)] + fetch, "tail", flops, moved,
    )
    output = call(
        functools.partial(output_kernel, act),
        jax.ShapeDtypeStruct((2, avir, act * pairs), F32), [VMEM] * 2, (), "output",
    )

    for step in range(PASSES):
        if step == 0:
            start, inverse, part, piece = first(
                source, eps_vir.reshape(avir, 1), eps_act, energy, own, other
            )
            state = start
        else:
            state, part, piece = later(recv, state, kron, start, inverse, own, other)
        mixed = exchange(along_z(exchange(part, "y"), piece), "z")
        inter = exchange(summed(mixed), "z")
        mixed = exchange(along_y(inter, coupled(mixed, couple)), "y")
        recv = exchange(tail(mixed, own, other), "x")
    state = last(recv, state, kron, start, inverse)
    return output(state, lax.ppermute(state, "c", swap))


def solution(mesh, sizes=(8, 4, 4, 2)):
    in_specs = (
        P(None, VIR, None, FIT),
        P(None, FIT, None),
        P(),
        P(VIR),
        P(),
        P(),
        P(None, VIR, None),
    )
    return jax.shard_map(
        per_device,
        mesh=Mesh(mesh.devices.reshape(*sizes), ("z", "y", "x", "c")),
        in_specs=in_specs,
        out_specs=P(None, VIR, None),
        check_vma=False,
    )
```

```python
import functools

import jax
import jax.numpy as jnp
from jax import lax
from jax.experimental import pallas as pl
from jax.experimental.pallas import tpu as pltpu
from jax.sharding import Mesh
from jax.sharding import PartitionSpec as P

PASSES = 3
VIR = ("z", "y")
FIT = ("x", "c")
F32 = jnp.float32
BF16 = jnp.bfloat16
LANES = 128
GROUP = 10
CHUNK = 512
VMEM_LIMIT = 60 << 20


def low_count(avir):
    return -(-avir // (2 * GROUP)) * GROUP


def lane(shape):
    return lax.broadcasted_iota(jnp.int32, shape, len(shape) - 1)


def turned(both):
    ahead = pltpu.roll(both, LANES - 32, 1)
    behind = pltpu.roll(both, 32, 1)
    return jnp.where((lane(both.shape) & 32) == 0, -ahead, behind)


def merged(left, right):
    first = lane(left.shape) < 64
    return (
        jnp.where(first, left, pltpu.roll(right, 64, 1)),
        jnp.where(first, pltpu.roll(left, 64, 1), right),
    )


def mxu(left, right, dims=((1,), (0,))):
    return lax.dot_general(left, right, (dims, ((), ())), preferred_element_type=F32)


def chunks(rows, width):
    out = []
    for half in range(2):
        end = rows if half == 0 else width - rows
        for at in range(0, end, CHUNK):
            out.append((half, at, min(at + CHUNK, end), half * rows + at))
    return out


def fetches(blocks, buf, sems, parts):
    copies = []
    for n, (_, at, end, row) in enumerate(parts):
        both = []
        for s, ref in enumerate(blocks):
            where = pl.ds(row, end - at)
            both.append(
                pltpu.make_async_copy(
                    ref.at[:, where, :], buf.at[s, :, where, :], sems.at[n, s]
                )
            )
        copies.append(both)
    for both in copies:
        for copy in both:
            copy.start()
    return copies


def tiles_per_row(nfit, vir_count):
    count = -(-nfit // LANES)
    while 16 * count % (2 * vir_count):
        count += 1
    return count


def active_term(prev_ref, kron, rows, act):
    block = GROUP * act
    parts = []
    for at in range(0, rows, block):
        value = prev_ref[at : at + block, :]
        head = value.astype(BF16)
        tail = (value - head.astype(F32)).astype(BF16)
        both = mxu(kron, jnp.concatenate([head, tail, head], axis=0))
        parts.append(both[:block] + turned(both[block:]))
    return jnp.concatenate(parts, axis=0)


def updated(recvs, prev_ref, kron_ref, start_ref, inv_ref, act):
    rows = start_ref.shape[0]
    values = [recv[...].astype(F32) for recv in recvs]
    while len(values) > 1:
        values = [values[i] + values[i + 1] for i in range(0, len(values), 2)]
    total = active_term(prev_ref, kron_ref[...], rows, act) + values[0]
    return start_ref[...] - total * inv_ref[...]


def set_share(state_ref, share_ref, act):
    low = state_ref.shape[0] // act
    count = share_ref.shape[0] // low
    first = lax.axis_index("x") * count
    for i in range(0, count, 2):
        both = [state_ref[pl.ds(first + i + k, low, stride=act), :] for k in range(2)]
        share_ref[i * low : (i + 2) * low, :] = jnp.concatenate(both, axis=0).astype(BF16)


def overlap(state_ref, pieces_ref, buf, copies, parts):
    across = state_ref[...].T
    flips = []
    plain = []
    for half in range(2):
        re = across[64 * half : 64 * half + 32]
        im = across[64 * half + 32 : 64 * half + 64]
        plain.append(jnp.concatenate([re, im], axis=0).astype(BF16))
        flips.append(jnp.concatenate([im, -re], axis=0).astype(BF16))
    count = buf.shape[0]
    sums = [None] * count
    for n, (half, at, end, row) in enumerate(parts):
        for s in range(count):
            copies[n][s].wait()
            here = mxu(plain[half][:, at:end], buf[s, 0, row : row + end - at, :])
            here += mxu(flips[half][:, at:end], buf[s, 1, row : row + end - at, :])
            sums[s] = here if sums[s] is None else sums[s] + here
    nfit = sums[0].shape[1]
    pieces, depth, _ = pieces_ref.shape
    groups = 8 * count
    wide = pieces * depth // (8 * groups)

    def tile(slot):
        group, k = divmod(slot, wide)
        if k * LANES >= nfit:
            return jnp.zeros((8, LANES), F32)
        s, at = divmod(group * 8, 64)
        return sums[s][at : at + 8, k * LANES : (k + 1) * LANES]

    for slot in range(0, groups * wide, 2):
        both = jnp.concatenate([tile(slot), tile(slot + 1)], axis=0).astype(BF16)
        piece, at = divmod(slot * 8, depth)
        pieces_ref[piece, at : at + 16, :] = both


def spread(pieces_ref, outs):
    me = lax.axis_index("y")
    for k, out in enumerate(outs):
        out[...] = pieces_ref[me ^ k]


def prepare(source_ref, vir_ref, act_ref, pair_ref, start_ref, inv_ref, act):
    core = lax.axis_index("c")
    avir = source_ref.shape[1]
    low = start_ref.shape[0] // act
    spare = 2 * low - avir
    at = lane((low, LANES))
    row = lax.broadcasted_iota(jnp.int32, (low, LANES), 0)
    held = (at < 64) | (row < low - spare)

    def lifted(values, fill):
        rest = jnp.full((spare, values.shape[1]), fill, F32)
        return values[:low], jnp.concatenate([values[low:], rest], axis=0)

    above = lifted(jnp.broadcast_to(vir_ref[...], (avir, LANES)), 1.0)
    above = jnp.where(at < 64, above[0], above[1]) - pair_ref[...]
    for pair in range(act // 2):
        sides = []
        for part in range(2):
            values = source_ref[part, :, pair * LANES : (pair + 1) * LANES]
            values = jnp.where(core == 0, values, pltpu.roll(values, LANES - 32, 1))
            sides += lifted(values, 0.0)
        order = (sides[0], sides[2], sides[1], sides[3])
        for k in range(2):
            t = 2 * pair + k
            value = None
            for n in (3, 2, 1, 0):
                shift = (32 * n - 64 * k) % LANES
                moved = pltpu.roll(order[n], shift, 1) if shift else order[n]
                value = moved if value is None else jnp.where(at < 32 * (n + 1), moved, value)
            inverse = jnp.where(held, 1.0 / (above + act_ref[t]), 0.0)
            inv_ref[pl.ds(t, low, stride=act), :] = inverse
            start_ref[pl.ds(t, low, stride=act), :] = value * inverse


def opening_kernel(
    act, source_ref, vir_ref, act_ref, pair_ref, own,
    start_ref, inv_ref, share_ref, pieces_ref, buf, sems,
):
    parts = chunks(start_ref.shape[0], own.shape[1])
    copies = fetches([own], buf, sems, parts)
    prepare(source_ref, vir_ref, act_ref, pair_ref, start_ref, inv_ref, act)
    set_share(start_ref, share_ref, act)
    overlap(start_ref, pieces_ref, buf, copies, parts)


def second_kernel(start_ref, first_ref, other, *rest):
    *outs, pieces, buf, sems = rest
    parts = chunks(start_ref.shape[0], other.shape[1])
    copies = fetches([other], buf, sems, parts)
    count = first_ref.shape[0]
    pieces[:count] = first_ref[...]
    overlap(start_ref, pieces.at[count:], buf, copies, parts)
    spread(pieces, outs)


def next_kernel(act, nx, *refs):
    recvs = refs[:nx]
    prev_ref, kron_ref, start_ref, inv_ref, own, other, state_ref, share_ref, *rest = refs[nx:]
    *outs, pieces, buf, sems = rest
    parts = chunks(start_ref.shape[0], own.shape[1])
    copies = fetches([own, other], buf, sems, parts)
    state_ref[...] = updated(recvs, prev_ref, kron_ref, start_ref, inv_ref, act)
    set_share(state_ref, share_ref, act)
    overlap(state_ref, pieces, buf, copies, parts)
    spread(pieces, outs)


def last_kernel(act, nx, *refs):
    prev_ref, kron_ref, start_ref, inv_ref, state_ref = refs[nx:]
    state_ref[...] = updated(refs[:nx], prev_ref, kron_ref, start_ref, inv_ref, act)


def kron_kernel(fock_ref, out_ref):
    act = fock_ref.shape[1]
    block = GROUP * act
    row = lax.broadcasted_iota(jnp.int32, (block, act), 0)
    col = lax.broadcasted_iota(jnp.int32, (block, act), 1)
    pick = jnp.where(lax.rem(row, act) == col, 1.0, 0.0).astype(BF16)
    row = lax.broadcasted_iota(jnp.int32, (block, block), 0)
    col = lax.broadcasted_iota(jnp.int32, (block, block), 1)
    same = lax.div(row, act) == lax.div(col, act)
    last = ((1,), (1,))
    for part in range(2):
        value = fock_ref[part]
        head = value.astype(BF16)
        rest = (value - head.astype(F32)).astype(BF16)
        tables = []
        for term in (head, rest):
            table = mxu(mxu(pick, term, last).astype(BF16), pick, last)
            tables.append(jnp.where(same, table, 0.0))
        out_ref[part * block : (part + 1) * block, :] = jnp.concatenate(
            [tables[0], tables[0], tables[1]], axis=1
        ).astype(BF16)


def output_kernel(act, mine_ref, theirs_ref, out_ref):
    core = lax.axis_index("c")
    avir = out_ref.shape[1]
    low = mine_ref.shape[0] // act
    at = lane((low, LANES))
    for pair in range(act // 2):
        order = []
        for k in range(2):
            where = pl.ds(2 * pair + k, low, stride=act)
            mine, theirs = mine_ref[where, :], theirs_ref[where, :]
            order.append(jnp.where(core == 0, mine, theirs))
            order.append(jnp.where(core == 0, theirs, mine))
        for side in range(2):
            for part in range(2):
                value = None
                for n in (3, 2, 1, 0):
                    shift = (32 * n - 64 * side - 32 * part) % LANES
                    moved = pltpu.roll(order[n], shift, 1) if shift else order[n]
                    value = moved if value is None else jnp.where(at < 32 * (n + 1), moved, value)
                rows = low if side == 0 else avir - low
                out_ref[part, pl.ds(side * low, rows), pair * LANES : (pair + 1) * LANES] = value[
                    :rows
                ]


def total_of(refs, at, rows):
    total = refs[0][at : at + rows, :].astype(F32)
    for ref in refs[1:]:
        total += ref[at : at + rows, :].astype(F32)
    return total


def along_z_kernel(*refs):
    *recvs, share_ref, out_ref = refs
    nz, rows, _ = out_ref.shape
    depth = rows - share_ref.shape[0]
    share = share_ref[...]
    for z in range(nz):
        out_ref[z, :depth, :] = total_of(recvs, z * depth, depth).astype(BF16)
        out_ref[z, depth:, :] = share


def sum_kernel(recv_ref, out_ref):
    nz, rows, _ = out_ref.shape
    total = total_of([recv_ref.at[z] for z in range(nz)], 0, rows).astype(BF16)
    for i in range(nz):
        out_ref[i] = total


def couple_kernel(recv_ref, couple_ref, out_ref):
    nz, height, _ = recv_ref.shape
    ny, rows, _ = out_ref.shape
    low = couple_ref.shape[1] // (2 * nz)
    base = height - rows
    couple = couple_ref[...]
    half = couple.shape[0] // 2
    for at in range(0, rows, 2 * low):
        lines = []
        for z in range(nz):
            both = recv_ref[z, base + at : base + at + 2 * low, :].astype(F32)
            lines += merged(both[:low], both[low:])
        both = mxu(couple, jnp.concatenate(lines, axis=0).astype(BF16))
        term = both[:half] + turned(both[half:])
        for y in range(ny):
            top = y * 2 * low
            pieces = merged(term[top : top + low], term[top + low : top + 2 * low])
            out_ref[y, at : at + 2 * low, :] = jnp.concatenate(pieces, axis=0).astype(BF16)


def along_y_kernel(inter_ref, vir_ref, *outs):
    nz, depth, _ = inter_ref.shape
    me = lax.axis_index("y")
    for k, out in enumerate(outs):
        for z in range(nz):
            out[z * depth : (z + 1) * depth, :] = inter_ref[z]
        out[nz * depth :, :] = vir_ref[me ^ k]


def tail_kernel(act, height, *refs):
    *recvs, own, other, out_ref, inter_ref, total, buf, sems = refs
    rows = total.shape[0]
    nfit = own.shape[2]
    parts = chunks(rows, own.shape[1])
    copies = fetches([own, other], buf, sems, parts)
    me = lax.axis_index("y")
    for k, recv in enumerate(recvs):
        inter_ref[me ^ k] = recv[:height, :]
    wide = inter_ref.shape[0] * height // LANES
    tiles = {}
    for slot in range(0, 16 * wide, 2):
        piece, at = divmod(slot * 8, height)
        both = inter_ref[piece, at : at + 16, :].astype(F32)
        tiles[slot], tiles[slot + 1] = both[:8], both[8:]
    count = -(-nfit // LANES)
    lines = [
        jnp.concatenate([tiles[g * wide + k] for k in range(count)], axis=1)
        for g in range(16)
    ]
    zero = jnp.zeros((64, nfit), F32)
    right = []
    for s in range(2):
        re = jnp.concatenate(lines[8 * s : 8 * s + 4], axis=0)
        im = jnp.concatenate(lines[8 * s + 4 : 8 * s + 8], axis=0)
        plain = jnp.concatenate([re, im], axis=0)
        turn = jnp.concatenate([-im, re], axis=0)
        right.append(
            [
                [jnp.concatenate(order, axis=0).astype(BF16) for order in ((v, zero), (zero, v))]
                for v in (plain, turn)
            ]
        )
    last = ((1,), (1,))
    for n, (half, at, end, row) in enumerate(parts):
        here = None
        for s in range(2):
            copies[n][s].wait()
            for k in range(2):
                term = mxu(buf[s, k, row : row + end - at, :], right[s][k][half], last)
                here = term if here is None else here + term
        if half:
            total[at:end, :] += here
        else:
            total[at:end, :] = here
    low = rows // act
    share = (recvs[0].shape[0] - height) // low
    first = lax.axis_index("x") * share
    for i in range(0, share, 2):
        both = total_of(recvs, height + i * low, 2 * low)
        for k in range(2):
            where = pl.ds(first + i + k, low, stride=act)
            total[where, :] = total[where, :] + both[k * low : (k + 1) * low]
    out_ref[...] = total[...].astype(BF16)


VMEM = pl.BlockSpec(memory_space=pltpu.VMEM)
HBM = pl.BlockSpec(memory_space=pltpu.HBM)
SMEM = pl.BlockSpec(memory_space=pltpu.SMEM)


def call(body, outs, ins, scratch=(), name=None, flops=0, moved=0):
    return pl.pallas_call(
        body,
        out_shape=outs,
        in_specs=ins,
        out_specs=jax.tree.map(lambda _: VMEM, outs),
        scratch_shapes=scratch,
        compiler_params=pltpu.CompilerParams(vmem_limit_bytes=VMEM_LIMIT),
        cost_estimate=pl.CostEstimate(flops=flops, bytes_accessed=moved, transcendentals=0),
        name=name,
    )


def exchange(copies, axis):
    return lax.all_to_all(copies, axis, 0, 0, tiled=True)


def swapped(values, axis):
    size = len(values)
    return [values[0]] + [
        lax.ppermute(values[k], axis, [(i, i ^ k) for i in range(size)]) for k in range(1, size)
    ]


def laid_out(couple, low, ny):
    nz, _, avir, _ = couple.shape
    couple = couple.reshape(nz, 2, avir, ny, avir)
    fill = (0, 2 * low - avir)
    couple = jnp.pad(couple, ((0, 0), (0, 0), fill, (0, 0), fill))
    return couple.transpose(1, 3, 4, 0, 2).reshape(4 * ny * low, 2 * nz * low)


def per_device(fitted, vcouple, actfock, eps_vir, eps_act, pair_energy, source):
    cores, nx, ny, nz = (lax.axis_size(n) for n in ("c", "x", "y", "z"))
    core = lax.axis_index("c")
    _, avir, act, nfit = fitted.shape
    pairs = pair_energy.shape[0]
    half = pairs // cores
    width = avir * act
    low = low_count(avir)
    rows = low * act
    share = act // nx
    swap = [(0, 1), (1, 0)]
    own = fitted.reshape(2, width, nfit)
    other = lax.ppermute(own, "c", swap)

    mine = lax.dynamic_slice_in_dim(vcouple, lax.axis_index("y") * avir, avir, 1)
    mine = lax.dynamic_slice_in_dim(mine, lax.axis_index("z") * avir * ny, avir * ny, 2)
    couple = exchange(jnp.broadcast_to(mine[None], (nz, *mine.shape)), FIT)

    energy = lax.dynamic_slice_in_dim(pair_energy, core * half, half, 0)
    energy = jnp.tile(energy, LANES // half).reshape(1, LANES)

    wide = tiles_per_row(nfit, ny * nz)
    height = 16 * wide * 8 // ny
    depth = height // nz
    extra = share * low

    def sent(*shape):
        return jax.ShapeDtypeStruct((*shape, LANES), BF16)

    state_shape = jax.ShapeDtypeStruct((rows, LANES), F32)
    piece_shape, share_shape = [sent(height)] * ny, sent(extra)
    pieces = pltpu.VMEM((ny, height, LANES), BF16)
    steps = len(chunks(rows, width))

    def fetch(count):
        return [
            pltpu.VMEM((count, 2, width, nfit), BF16), pltpu.SemaphoreType.DMA((steps, count))
        ]

    flops = 16 * width * nfit * 32
    moved = 8 * width * nfit
    opening = call(
        functools.partial(opening_kernel, act),
        [state_shape, state_shape, share_shape, sent(ny // 2, height)],
        [VMEM, VMEM, SMEM, VMEM, HBM], fetch(1), "opening", flops // 2, moved // 2,
    )
    second = call(
        second_kernel, piece_shape, [VMEM, VMEM, HBM], [pieces] + fetch(1), "second",
        flops // 2, moved // 2,
    )
    later = call(
        functools.partial(next_kernel, act, nx), [state_shape, share_shape] + piece_shape,
        [VMEM] * (nx + 4) + [HBM] * 2, [pieces] + fetch(2), "later", flops, moved,
    )
    last = call(
        functools.partial(last_kernel, act, nx), state_shape, [VMEM] * (nx + 4), (), "last"
    )
    block = GROUP * act
    kron = call(
        kron_kernel, jax.ShapeDtypeStruct((2 * block, 3 * block), BF16), [VMEM], (), "kron"
    )(actfock)
    along_z = call(
        along_z_kernel, sent(nz, depth + extra), [VMEM] * (ny + 1), (), "along_z"
    )
    summed = call(sum_kernel, sent(nz, depth), [VMEM], (), "summed")
    coupled = call(couple_kernel, sent(ny, extra), [VMEM] * 2, (), "coupled")
    along_y = call(
        along_y_kernel, [sent(height + extra)] * ny, [VMEM] * 2, (), "along_y"
    )
    tail = call(
        functools.partial(tail_kernel, act, height), sent(rows),
        [VMEM] * ny + [HBM] * 2, [pieces, pltpu.VMEM((rows, LANES), F32)] + fetch(2), "tail", flops, moved,
    )
    output = call(
        functools.partial(output_kernel, act),
        jax.ShapeDtypeStruct((2, avir, act * pairs), F32), [VMEM] * 2, (), "output",
    )

    for step in range(PASSES):
        if step == 0:
            start, inverse, share_now, part = opening(
                source, eps_vir.reshape(avir, 1), eps_act, energy, own
            )
            state = start
            part = second(start, part, other)
            part, couple = lax.optimization_barrier((part, couple))
            couple = laid_out(couple, low, ny)
        else:
            state, share_now, *part = later(*recv, state, kron, start, inverse, own, other)
        mixed = exchange(along_z(*swapped(part, "y"), share_now), "z")
        inter = exchange(summed(mixed), "z")
        mixed = swapped(along_y(inter, coupled(mixed, couple)), "y")
        recv = swapped([tail(*mixed, own, other)] * nx, "x")
    state = last(*recv, state, kron, start, inverse)
    return output(state, lax.ppermute(state, "c", swap))


def solution(mesh, sizes=(8, 4, 4, 2)):
    in_specs = (
        P(None, VIR, None, FIT),
        P(None, FIT, None),
        P(),
        P(VIR),
        P(),
        P(),
        P(None, VIR, None),
    )
    return jax.shard_map(
        per_device,
        mesh=Mesh(mesh.devices.reshape(*sizes), ("z", "y", "x", "c")),
        in_specs=in_specs,
        out_specs=P(None, VIR, None),
        check_vma=False,
    )
```

```python
import functools

import jax
import jax.numpy as jnp
from jax import lax
from jax.experimental import pallas as pl
from jax.experimental.pallas import tpu as pltpu
from jax.sharding import Mesh
from jax.sharding import PartitionSpec as P

PASSES = 3
VIR = ("z", "y")
FIT = ("x", "c")
F32 = jnp.float32
BF16 = jnp.bfloat16
LANES = 128
GROUP = 10
CHUNK = 256
STRIPS = 4
LARGE = 36 << 20
SMALL = 12 << 20


def low_count(avir):
    return -(-avir // (2 * GROUP)) * GROUP


def lane(shape):
    return lax.broadcasted_iota(jnp.int32, shape, len(shape) - 1)


def turned(both):
    ahead = pltpu.roll(both, LANES - 32, 1)
    behind = pltpu.roll(both, 32, 1)
    return jnp.where((lane(both.shape) & 32) == 0, -ahead, behind)


def merged(left, right):
    first = lane(left.shape) < 64
    return (
        jnp.where(first, left, pltpu.roll(right, 64, 1)),
        jnp.where(first, pltpu.roll(left, 64, 1), right),
    )


def mxu(left, right, dims=((1,), (0,))):
    return lax.dot_general(left, right, (dims, ((), ())), preferred_element_type=F32)


def steps_of(rows):
    return -(-rows // CHUNK)


def buffer_rows(rows):
    return rows + steps_of(rows) * CHUNK


def strips(rows, width):
    depth = 2 * rows // STRIPS
    return [[(at, min(at + depth, width))] for at in range(0, width, depth)]


def pairs_of(rows, width):
    out = []
    for at in range(0, rows, CHUNK):
        ends = ((at, min(at + CHUNK, rows)), (rows + at, min(rows + at + CHUNK, width)))
        out.append([(first, end) for first, end in ends if end > first])
    return out


def fetches(blocks, buf, sems, plan):
    width = blocks[0].shape[1]
    buf[:, :, width:, :] = jnp.zeros(
        (buf.shape[0], 2, buf.shape[2] - width, buf.shape[3]), BF16
    )
    copies = []
    for n, ranges in enumerate(plan):
        step = []
        for s, ref in enumerate(blocks):
            for k, (first, end) in enumerate(ranges):
                where = pl.ds(first, end - first)
                step.append(
                    pltpu.make_async_copy(
                        ref.at[:, where, :], buf.at[s, :, where, :], sems.at[n, s, k]
                    )
                )
        copies.append(step)
    for step in copies:
        for copy in step:
            copy.start()
    return copies


def wait_for(copies, n):
    for i, step in enumerate(copies):

        @pl.when(n == i)
        def _():
            for copy in step:
                copy.wait()


def tiles_per_row(nfit, vir_count):
    count = -(-nfit // LANES)
    while 16 * count % (2 * vir_count):
        count += 1
    return count


def set_updated(state_ref, recvs, prev_ref, kron_ref, start_ref, inv_ref, act):
    block = GROUP * act

    @pl.loop(0, start_ref.shape[0] // block, unroll=2 if start_ref.shape[0] % (2 * block) == 0 else 1)
    def _(n):
        where = pl.ds(pl.multiple_of(n * block, block), block)
        value = prev_ref[where, :]
        head = value.astype(BF16)
        tail = (value - head.astype(F32)).astype(BF16)
        both = mxu(kron_ref[...], jnp.concatenate([head, tail, head], axis=0))
        values = [recv[where, :].astype(F32) for recv in recvs]
        while len(values) > 1:
            values = [values[i] + values[i + 1] for i in range(0, len(values), 2)]
        total = both[:block] + turned(both[block:]) + values[0]
        state_ref[where, :] = start_ref[where, :] - total * inv_ref[where, :]


def set_share(state_ref, share_ref, act):
    low = state_ref.shape[0] // act
    count = share_ref.shape[0] // low
    first = lax.axis_index("x") * count
    for i in range(0, count, 2):
        both = [state_ref[pl.ds(first + i + k, low, stride=act), :] for k in range(2)]
        share_ref[i * low : (i + 2) * low, :] = jnp.concatenate(both, axis=0).astype(BF16)


def overlap(state_ref, pieces_ref, buf, acc, across, copies):
    rows = state_ref.shape[0]
    value = state_ref[...].T
    spare = jnp.zeros((64, across.shape[3] - rows), F32)
    for half in range(2):
        re = value[64 * half : 64 * half + 32]
        im = value[64 * half + 32 : 64 * half + 64]
        for k, order in enumerate(((re, im), (im, -re))):
            both = jnp.concatenate([jnp.concatenate(order, axis=0), spare], axis=1)
            across[half, k] = both.astype(BF16)
    count = buf.shape[0]
    acc[...] = jnp.zeros(acc.shape, F32)

    @pl.loop(0, len(copies))
    def _(n):
        wait_for(copies, n)
        here = pl.ds(pl.multiple_of(n * CHUNK, CHUNK), CHUNK)
        left = [[across[half, k, :, here] for k in range(2)] for half in range(2)]
        for s in range(count):
            total = None
            for half in range(2):
                there = pl.ds(pl.multiple_of(half * rows + n * CHUNK, 16), CHUNK)
                for k in range(2):
                    term = mxu(left[half][k], buf[s, k, there, :])
                    total = term if total is None else total + term
            acc[s] += total

    sums = [acc[s] for s in range(count)]
    nfit = sums[0].shape[1]
    pieces, depth, _ = pieces_ref.shape
    groups = 8 * count
    wide = pieces * depth // (8 * groups)

    def tile(slot):
        group, k = divmod(slot, wide)
        if k * LANES >= nfit:
            return jnp.zeros((8, LANES), F32)
        s, at = divmod(group * 8, 64)
        return sums[s][at : at + 8, k * LANES : (k + 1) * LANES]

    for slot in range(0, groups * wide, 2):
        both = jnp.concatenate([tile(slot), tile(slot + 1)], axis=0).astype(BF16)
        piece, at = divmod(slot * 8, depth)
        pieces_ref[piece, at : at + 16, :] = both


def spread(pieces_ref, outs):
    me = lax.axis_index("y")
    for k, out in enumerate(outs):
        out[...] = pieces_ref[me ^ k]


def prepare(source_ref, vir_ref, act_ref, pair_ref, start_ref, inv_ref, act):
    core = lax.axis_index("c")
    avir = source_ref.shape[1]
    low = start_ref.shape[0] // act
    spare = 2 * low - avir
    at = lane((low, LANES))
    row = lax.broadcasted_iota(jnp.int32, (low, LANES), 0)
    held = (at < 64) | (row < low - spare)

    def lifted(values, fill):
        rest = jnp.full((spare, values.shape[1]), fill, F32)
        return values[:low], jnp.concatenate([values[low:], rest], axis=0)

    above = lifted(jnp.broadcast_to(vir_ref[...], (avir, LANES)), 1.0)
    above = jnp.where(at < 64, above[0], above[1]) - pair_ref[...]

    @pl.loop(0, act // 2, unroll=3)
    def _(pair):
        sides = []
        for part in range(2):
            where = pl.ds(pl.multiple_of(pair * LANES, LANES), LANES)
            values = source_ref[part, :, where]
            values = jnp.where(core == 0, values, pltpu.roll(values, LANES - 32, 1))
            sides += lifted(values, 0.0)
        order = (sides[0], sides[2], sides[1], sides[3])
        for k in range(2):
            t = 2 * pair + k
            value = None
            for n in (3, 2, 1, 0):
                shift = (32 * n - 64 * k) % LANES
                moved = pltpu.roll(order[n], shift, 1) if shift else order[n]
                value = moved if value is None else jnp.where(at < 32 * (n + 1), moved, value)
            inverse = jnp.where(held, 1.0 / (above + act_ref[t]), 0.0)
            inv_ref[pl.ds(t, low, stride=act), :] = inverse
            start_ref[pl.ds(t, low, stride=act), :] = value * inverse


def opening_kernel(
    act, source_ref, vir_ref, act_ref, pair_ref, own,
    start_ref, inv_ref, share_ref, pieces_ref, *scratch,
):
    buf, sems, acc, across = scratch
    copies = fetches([own], buf, sems, pairs_of(start_ref.shape[0], own.shape[1]))
    prepare(source_ref, vir_ref, act_ref, pair_ref, start_ref, inv_ref, act)
    set_share(start_ref, share_ref, act)
    overlap(start_ref, pieces_ref, buf, acc, across, copies)


def second_kernel(start_ref, first_ref, other, *rest):
    *outs, pieces, buf, sems, acc, across = rest
    copies = fetches([other], buf, sems, pairs_of(start_ref.shape[0], other.shape[1]))
    count = first_ref.shape[0]
    pieces[:count] = first_ref[...]
    overlap(start_ref, pieces.at[count:], buf, acc, across, copies)
    spread(pieces, outs)


def next_kernel(act, nx, *refs):
    prev_ref, kron_ref, start_ref, inv_ref, own, other, state_ref, share_ref, *rest = refs[nx:]
    *outs, pieces, buf, sems, acc, across = rest
    copies = fetches([own, other], buf, sems, pairs_of(start_ref.shape[0], own.shape[1]))
    set_updated(state_ref, refs[:nx], prev_ref, kron_ref, start_ref, inv_ref, act)
    set_share(state_ref, share_ref, act)
    overlap(state_ref, pieces, buf, acc, across, copies)
    spread(pieces, outs)


def last_kernel(act, nx, *refs):
    prev_ref, kron_ref, start_ref, inv_ref, state_ref = refs[nx:]
    set_updated(state_ref, refs[:nx], prev_ref, kron_ref, start_ref, inv_ref, act)


def kron_kernel(fock_ref, out_ref):
    act = fock_ref.shape[1]
    block = GROUP * act
    row = lax.broadcasted_iota(jnp.int32, (block, act), 0)
    col = lax.broadcasted_iota(jnp.int32, (block, act), 1)
    pick = jnp.where(lax.rem(row, act) == col, 1.0, 0.0).astype(BF16)
    row = lax.broadcasted_iota(jnp.int32, (block, block), 0)
    col = lax.broadcasted_iota(jnp.int32, (block, block), 1)
    same = lax.div(row, act) == lax.div(col, act)
    last = ((1,), (1,))
    for part in range(2):
        value = fock_ref[part]
        head = value.astype(BF16)
        rest = (value - head.astype(F32)).astype(BF16)
        tables = []
        for term in (head, rest):
            table = mxu(mxu(pick, term, last).astype(BF16), pick, last)
            tables.append(jnp.where(same, table, 0.0))
        out_ref[part * block : (part + 1) * block, :] = jnp.concatenate(
            [tables[0], tables[0], tables[1]], axis=1
        ).astype(BF16)


def output_kernel(act, mine_ref, theirs_ref, out_ref):
    core = lax.axis_index("c")
    avir = out_ref.shape[1]
    low = mine_ref.shape[0] // act
    at = lane((low, LANES))

    @pl.loop(0, act // 2, unroll=3)
    def _(pair):
        order = []
        for k in range(2):
            where = pl.ds(2 * pair + k, low, stride=act)
            mine, theirs = mine_ref[where, :], theirs_ref[where, :]
            order.append(jnp.where(core == 0, mine, theirs))
            order.append(jnp.where(core == 0, theirs, mine))
        for side in range(2):
            for part in range(2):
                value = None
                for n in (3, 2, 1, 0):
                    shift = (32 * n - 64 * side - 32 * part) % LANES
                    moved = pltpu.roll(order[n], shift, 1) if shift else order[n]
                    value = moved if value is None else jnp.where(at < 32 * (n + 1), moved, value)
                rows = low if side == 0 else avir - low
                where = pl.ds(pl.multiple_of(pair * LANES, LANES), LANES)
                out_ref[part, pl.ds(side * low, rows), where] = value[:rows]


def total_of(refs, at, rows):
    total = refs[0][at : at + rows, :].astype(F32)
    for ref in refs[1:]:
        total += ref[at : at + rows, :].astype(F32)
    return total


def along_z_kernel(*refs):
    *recvs, share_ref, out_ref = refs
    nz, rows, _ = out_ref.shape
    depth = rows - share_ref.shape[0]
    share = share_ref[...]
    for z in range(nz):
        out_ref[z, :depth, :] = total_of(recvs, z * depth, depth).astype(BF16)
        out_ref[z, depth:, :] = share


def sum_kernel(recv_ref, out_ref):
    nz, rows, _ = out_ref.shape
    total = total_of([recv_ref.at[z] for z in range(nz)], 0, rows).astype(BF16)
    for i in range(nz):
        out_ref[i] = total


def couple_kernel(recv_ref, couple_ref, out_ref):
    nz, height, _ = recv_ref.shape
    ny, rows, _ = out_ref.shape
    low = couple_ref.shape[1] // (2 * nz)
    base = height - rows
    couple = couple_ref[...]
    half = couple.shape[0] // 2

    @pl.loop(0, rows // (2 * low))
    def _(n):
        at = pl.multiple_of(n * 2 * low, 16)
        lines = []
        for z in range(nz):
            there = pl.ds(pl.multiple_of(base + n * 2 * low, 16), 2 * low)
            both = recv_ref[z, there, :].astype(F32)
            lines += merged(both[:low], both[low:])
        both = mxu(couple, jnp.concatenate(lines, axis=0).astype(BF16))
        term = both[:half] + turned(both[half:])
        for y in range(ny):
            top = y * 2 * low
            pieces = merged(term[top : top + low], term[top + low : top + 2 * low])
            out_ref[y, pl.ds(at, 2 * low), :] = jnp.concatenate(pieces, axis=0).astype(BF16)


def along_y_kernel(inter_ref, vir_ref, *outs):
    nz, depth, _ = inter_ref.shape
    me = lax.axis_index("y")
    for k, out in enumerate(outs):
        for z in range(nz):
            out[z * depth : (z + 1) * depth, :] = inter_ref[z]
        out[nz * depth :, :] = vir_ref[me ^ k]


def tail_kernel(act, height, *refs):
    *recvs, own, other, out_ref, inter_ref, both, total, right, recv_sems, buf, sems = refs
    rows = out_ref.shape[0]
    nfit = own.shape[2]
    me = lax.axis_index("y")
    moves = [
        pltpu.make_async_copy(recv, inter_ref.at[me ^ k], recv_sems.at[k])
        for k, recv in enumerate(recvs)
    ]
    for move in moves:
        move.start()
    copies = fetches([own, other], buf, sems, strips(rows, own.shape[1]))
    for move in moves:
        move.wait()
    wide = inter_ref.shape[0] * height // LANES
    tiles = {}
    for slot in range(0, 16 * wide, 2):
        piece, at = divmod(slot * 8, height)
        pair = inter_ref[piece, at : at + 16, :].astype(F32)
        tiles[slot], tiles[slot + 1] = pair[:8], pair[8:]
    count = -(-nfit // LANES)
    lines = [
        jnp.concatenate([tiles[g * wide + k] for k in range(count)], axis=1)
        for g in range(16)
    ]
    for s in range(2):
        re = jnp.concatenate(lines[8 * s : 8 * s + 4], axis=0)
        im = jnp.concatenate(lines[8 * s + 4 : 8 * s + 8], axis=0)
        for k, order in enumerate(((re, im), (-im, re))):
            right[s, k] = jnp.concatenate([*order, *order], axis=0).astype(BF16)

    depth = 2 * rows // STRIPS

    @pl.loop(0, len(copies))
    def _(n):
        wait_for(copies, n)
        there = pl.ds(pl.multiple_of(n * depth, 16), depth)
        here = None
        for s in range(2):
            for k in range(2):
                term = mxu(buf[s, k, there, :], right[s, k], ((1,), (1,)))
                here = term if here is None else here + term
        both[there, :] = here

    first_half = lane((rows, LANES)) < 64
    total[...] = jnp.where(first_half, both[:rows, :], both[rows:, :])
    low = rows // act
    share = (inter_ref.shape[1] - height) // low
    held = [inter_ref.at[y] for y in range(inter_ref.shape[0])]
    first = lax.axis_index("x") * share
    for i in range(0, share, 2):
        pair = total_of(held, height + i * low, 2 * low)
        for k in range(2):
            where = pl.ds(first + i + k, low, stride=act)
            total[where, :] = total[where, :] + pair[k * low : (k + 1) * low]
    out_ref[...] = total[...].astype(BF16)


VMEM = pl.BlockSpec(memory_space=pltpu.VMEM)
HBM = pl.BlockSpec(memory_space=pltpu.HBM)
SMEM = pl.BlockSpec(memory_space=pltpu.SMEM)


def call(body, outs, ins, scratch=(), name=None, flops=0, moved=0):
    return pl.pallas_call(
        body,
        out_shape=outs,
        in_specs=ins,
        out_specs=jax.tree.map(lambda _: VMEM, outs),
        scratch_shapes=scratch,
        compiler_params=pltpu.CompilerParams(vmem_limit_bytes=LARGE if flops else SMALL),
        cost_estimate=pl.CostEstimate(flops=flops, bytes_accessed=moved, transcendentals=0),
        name=name,
    )


def exchange(copies, axis):
    return lax.all_to_all(copies, axis, 0, 0, tiled=True)


def swapped(values, axis):
    size = len(values)
    return [values[0]] + [
        lax.ppermute(values[k], axis, [(i, i ^ k) for i in range(size)]) for k in range(1, size)
    ]


def laid_out(couple, low, ny):
    nz, _, avir, _ = couple.shape
    couple = couple.reshape(nz, 2, avir, ny, avir)
    fill = (0, 2 * low - avir)
    couple = jnp.pad(couple, ((0, 0), (0, 0), fill, (0, 0), fill))
    return couple.transpose(1, 3, 4, 0, 2).reshape(4 * ny * low, 2 * nz * low)


def per_device(fitted, vcouple, actfock, eps_vir, eps_act, pair_energy, source):
    cores, nx, ny, nz = (lax.axis_size(n) for n in ("c", "x", "y", "z"))
    core = lax.axis_index("c")
    _, avir, act, nfit = fitted.shape
    pairs = pair_energy.shape[0]
    half = pairs // cores
    width = avir * act
    low = low_count(avir)
    rows = low * act
    share = act // nx
    swap = [(0, 1), (1, 0)]
    own = fitted.reshape(2, width, nfit)
    other = lax.ppermute(own, "c", swap)

    mine = lax.dynamic_slice_in_dim(vcouple, lax.axis_index("y") * avir, avir, 1)
    mine = lax.dynamic_slice_in_dim(mine, lax.axis_index("z") * avir * ny, avir * ny, 2)
    couple = exchange(jnp.broadcast_to(mine[None], (nz, *mine.shape)), FIT)

    energy = lax.dynamic_slice_in_dim(pair_energy, core * half, half, 0)
    energy = jnp.tile(energy, LANES // half).reshape(1, LANES)

    wide = tiles_per_row(nfit, ny * nz)
    height = 16 * wide * 8 // ny
    depth = height // nz
    extra = share * low

    def sent(*shape):
        return jax.ShapeDtypeStruct((*shape, LANES), BF16)

    state_shape = jax.ShapeDtypeStruct((rows, LANES), F32)
    piece_shape, share_shape = [sent(height)] * ny, sent(extra)
    pieces = pltpu.VMEM((ny, height, LANES), BF16)
    steps = steps_of(rows)

    def fetch(count):
        return [
            pltpu.VMEM((count, 2, buffer_rows(rows), nfit), BF16),
            pltpu.SemaphoreType.DMA((max(steps, STRIPS), count, 2)),
        ]

    def sums(count):
        return fetch(count) + [
            pltpu.VMEM((count, 64, nfit), F32), pltpu.VMEM((2, 2, 64, steps * CHUNK), BF16)
        ]

    flops = 16 * width * nfit * 32
    moved = 8 * width * nfit
    opening = call(
        functools.partial(opening_kernel, act),
        [state_shape, state_shape, share_shape, sent(ny // 2, height)],
        [VMEM, VMEM, SMEM, VMEM, HBM], sums(1), "opening", flops // 2, moved // 2,
    )
    second = call(
        second_kernel, piece_shape, [VMEM, VMEM, HBM], [pieces] + sums(1), "second",
        flops // 2, moved // 2,
    )
    later = call(
        functools.partial(next_kernel, act, nx), [state_shape, share_shape] + piece_shape,
        [VMEM] * (nx + 4) + [HBM] * 2, [pieces] + sums(2), "later", flops, moved,
    )
    last = call(
        functools.partial(last_kernel, act, nx), state_shape, [VMEM] * (nx + 4), (), "last"
    )
    block = GROUP * act
    kron = call(
        kron_kernel, jax.ShapeDtypeStruct((2 * block, 3 * block), BF16), [VMEM], (), "kron"
    )(actfock)
    along_z = call(
        along_z_kernel, sent(nz, depth + extra), [VMEM] * (ny + 1), (), "along_z"
    )
    summed = call(sum_kernel, sent(nz, depth), [VMEM], (), "summed")
    coupled = call(couple_kernel, sent(ny, extra), [VMEM] * 2, (), "coupled")
    along_y = call(
        along_y_kernel, [sent(height + extra)] * ny, [VMEM] * 2, (), "along_y"
    )
    tail = call(
        functools.partial(tail_kernel, act, height), sent(rows),
        [HBM] * (ny + 2),
        [
            pltpu.VMEM((ny, height + extra, LANES), BF16),
            pltpu.VMEM((2 * rows, LANES), F32),
            pltpu.VMEM((rows, LANES), F32),
            pltpu.VMEM((2, 2, LANES, nfit), BF16),
            pltpu.SemaphoreType.DMA((ny,)),
        ]
        + fetch(2),
        "tail", flops, moved,
    )
    output = call(
        functools.partial(output_kernel, act),
        jax.ShapeDtypeStruct((2, avir, act * pairs), F32), [VMEM] * 2, (), "output",
    )

    for step in range(PASSES):
        if step == 0:
            start, inverse, share_now, part = opening(
                source, eps_vir.reshape(avir, 1), eps_act, energy, own
            )
            state = start
            part = second(start, part, other)
            part, couple = lax.optimization_barrier((part, couple))
            couple = laid_out(couple, low, ny)
        else:
            state, share_now, *part = later(*recv, state, kron, start, inverse, own, other)
        mixed = exchange(along_z(*swapped(part, "y"), share_now), "z")
        inter = exchange(summed(mixed), "z")
        mixed = swapped(along_y(inter, coupled(mixed, couple)), "y")
        recv = swapped([tail(*mixed, own, other)] * nx, "x")
    state = last(*recv, state, kron, start, inverse)
    return output(state, lax.ppermute(state, "c", swap))


def solution(mesh, sizes=(8, 4, 4, 2)):
    in_specs = (
        P(None, VIR, None, FIT),
        P(None, FIT, None),
        P(),
        P(VIR),
        P(),
        P(),
        P(None, VIR, None),
    )
    return jax.shard_map(
        per_device,
        mesh=Mesh(mesh.devices.reshape(*sizes), ("z", "y", "x", "c")),
        in_specs=in_specs,
        out_specs=P(None, VIR, None),
        check_vma=False,
    )
```

```python
import functools

import jax
import jax.numpy as jnp
from jax import lax
from jax.experimental import pallas as pl
from jax.experimental.pallas import tpu as pltpu
from jax.sharding import Mesh
from jax.sharding import PartitionSpec as P

PASSES = 3
VIR = ("z", "y")
FIT = ("x", "c")
F32 = jnp.float32
BF16 = jnp.bfloat16
LANES = 128
GROUP = 10
CHUNK = 256
STRIPS = 4
LARGE = 36 << 20
MIDDLE = 20 << 20
SMALL = 12 << 20


def low_count(avir):
    return -(-avir // (2 * GROUP)) * GROUP


def lane(shape):
    return lax.broadcasted_iota(jnp.int32, shape, len(shape) - 1)


def turned(both):
    ahead = pltpu.roll(both, LANES - 32, 1)
    behind = pltpu.roll(both, 32, 1)
    return jnp.where((lane(both.shape) & 32) == 0, -ahead, behind)


def merged(left, right):
    first = lane(left.shape) < 64
    return (
        jnp.where(first, left, pltpu.roll(right, 64, 1)),
        jnp.where(first, pltpu.roll(left, 64, 1), right),
    )


def mxu(left, right, dims=((1,), (0,))):
    return lax.dot_general(left, right, (dims, ((), ())), preferred_element_type=F32)


def steps_of(rows):
    return -(-rows // CHUNK)


def buffer_rows(rows):
    return rows + steps_of(rows) * CHUNK


def pairs_of(rows, width):
    out = []
    for at in range(0, rows, CHUNK):
        ends = ((at, min(at + CHUNK, rows)), (rows + at, min(rows + at + CHUNK, width)))
        out.append([(first, end) for first, end in ends if end > first])
    return out


def fetches(blocks, buf, sems, plan):
    width = blocks[0].shape[1]
    buf[:, :, width:, :] = jnp.zeros(
        (buf.shape[0], 2, buf.shape[2] - width, buf.shape[3]), BF16
    )
    copies = []
    for n, ranges in enumerate(plan):
        step = []
        for s, ref in enumerate(blocks):
            for k, (first, end) in enumerate(ranges):
                where = pl.ds(first, end - first)
                step.append(
                    pltpu.make_async_copy(
                        ref.at[:, where, :], buf.at[s, :, where, :], sems.at[n, s, k]
                    )
                )
        copies.append(step)
    for step in copies:
        for copy in step:
            copy.start()
    return copies


def wait_for(copies, n):
    for i, step in enumerate(copies):

        @pl.when(n == i)
        def _():
            for copy in step:
                copy.wait()


def tiles_per_row(nfit, vir_count):
    count = -(-nfit // LANES)
    while 16 * count % (2 * vir_count):
        count += 1
    return count


def set_updated(state_ref, recvs, prev_ref, kron_ref, start_ref, inv_ref, act):
    block = GROUP * act

    @pl.loop(0, start_ref.shape[0] // block, unroll=2 if start_ref.shape[0] % (2 * block) == 0 else 1)
    def _(n):
        where = pl.ds(pl.multiple_of(n * block, block), block)
        value = prev_ref[where, :]
        head = value.astype(BF16)
        tail = (value - head.astype(F32)).astype(BF16)
        both = mxu(kron_ref[...], jnp.concatenate([head, tail, head], axis=0))
        values = [recv[where, :].astype(F32) for recv in recvs]
        while len(values) > 1:
            values = [values[i] + values[i + 1] for i in range(0, len(values), 2)]
        total = both[:block] + turned(both[block:]) + values[0]
        state_ref[where, :] = start_ref[where, :] - total * inv_ref[where, :]


def set_share(state_ref, share_ref, act):
    low = state_ref.shape[0] // act
    count = share_ref.shape[0] // low
    first = lax.axis_index("x") * count
    for i in range(0, count, 2):
        both = [state_ref[pl.ds(first + i + k, low, stride=act), :] for k in range(2)]
        share_ref[i * low : (i + 2) * low, :] = jnp.concatenate(both, axis=0).astype(BF16)


def overlap(state_ref, pieces_ref, buf, acc, across, copies=()):
    rows = state_ref.shape[0]
    value = state_ref[...].T
    spare = jnp.zeros((64, across.shape[3] - rows), F32)
    for half in range(2):
        re = value[64 * half : 64 * half + 32]
        im = value[64 * half + 32 : 64 * half + 64]
        for k, order in enumerate(((re, im), (im, -re))):
            both = jnp.concatenate([jnp.concatenate(order, axis=0), spare], axis=1)
            across[half, k] = both.astype(BF16)
    count = buf.shape[0]
    acc[...] = jnp.zeros(acc.shape, F32)

    @pl.loop(0, steps_of(rows))
    def _(n):
        wait_for(copies, n)
        here = pl.ds(pl.multiple_of(n * CHUNK, CHUNK), CHUNK)
        left = [[across[half, k, :, here] for k in range(2)] for half in range(2)]
        for s in range(count):
            total = None
            for half in range(2):
                there = pl.ds(pl.multiple_of(half * rows + n * CHUNK, 16), CHUNK)
                for k in range(2):
                    term = mxu(left[half][k], buf[s, k, there, :])
                    total = term if total is None else total + term
            acc[s] += total

    sums = [acc[s] for s in range(count)]
    nfit = sums[0].shape[1]
    pieces, depth, _ = pieces_ref.shape
    groups = 8 * count
    wide = pieces * depth // (8 * groups)

    def tile(slot):
        group, k = divmod(slot, wide)
        if k * LANES >= nfit:
            return jnp.zeros((8, LANES), F32)
        s, at = divmod(group * 8, 64)
        return sums[s][at : at + 8, k * LANES : (k + 1) * LANES]

    for slot in range(0, groups * wide, 2):
        both = jnp.concatenate([tile(slot), tile(slot + 1)], axis=0).astype(BF16)
        piece, at = divmod(slot * 8, depth)
        pieces_ref[piece, at : at + 16, :] = both


def spread(pieces_ref, outs):
    me = lax.axis_index("y")
    for k, out in enumerate(outs):
        out[...] = pieces_ref[me ^ k]


def prepare(source_ref, vir_ref, act_ref, pair_ref, start_ref, inv_ref, act):
    core = lax.axis_index("c")
    avir = source_ref.shape[1]
    low = start_ref.shape[0] // act
    spare = 2 * low - avir
    at = lane((low, LANES))
    row = lax.broadcasted_iota(jnp.int32, (low, LANES), 0)
    held = (at < 64) | (row < low - spare)

    def lifted(values, fill):
        rest = jnp.full((spare, values.shape[1]), fill, F32)
        return values[:low], jnp.concatenate([values[low:], rest], axis=0)

    above = lifted(jnp.broadcast_to(vir_ref[...], (avir, LANES)), 1.0)
    above = jnp.where(at < 64, above[0], above[1]) - pair_ref[...]

    @pl.loop(0, act // 2, unroll=3)
    def _(pair):
        sides = []
        for part in range(2):
            where = pl.ds(pl.multiple_of(pair * LANES, LANES), LANES)
            values = source_ref[part, :, where]
            values = jnp.where(core == 0, values, pltpu.roll(values, LANES - 32, 1))
            sides += lifted(values, 0.0)
        order = (sides[0], sides[2], sides[1], sides[3])
        for k in range(2):
            t = 2 * pair + k
            value = None
            for n in (3, 2, 1, 0):
                shift = (32 * n - 64 * k) % LANES
                moved = pltpu.roll(order[n], shift, 1) if shift else order[n]
                value = moved if value is None else jnp.where(at < 32 * (n + 1), moved, value)
            inverse = jnp.where(held, 1.0 / (above + act_ref[t]), 0.0)
            inv_ref[pl.ds(t, low, stride=act), :] = inverse
            start_ref[pl.ds(t, low, stride=act), :] = value * inverse


def stage_kernel(after, own, other, buf, zeros, sems):
    width = own.shape[1]
    zeros[...] = jnp.zeros(zeros.shape, BF16)
    copies = []
    for s, ref in enumerate((own, other)):
        copies.append(pltpu.make_async_copy(ref, buf.at[s, :, pl.ds(0, width), :], sems.at[s, 0]))
        there = buf.at[s, :, pl.ds(width, zeros.shape[1]), :]
        copies.append(pltpu.make_async_copy(zeros, there, sems.at[s, 1]))
    for copy in copies:
        copy.start()
    for copy in copies:
        copy.wait()


def opening_kernel(
    act, source_ref, vir_ref, act_ref, pair_ref, own,
    start_ref, inv_ref, share_ref, pieces_ref, *scratch,
):
    buf, sems, acc, across = scratch
    copies = fetches([own], buf, sems, pairs_of(start_ref.shape[0], own.shape[1]))
    prepare(source_ref, vir_ref, act_ref, pair_ref, start_ref, inv_ref, act)
    set_share(start_ref, share_ref, act)
    overlap(start_ref, pieces_ref, buf, acc, across, copies)


def second_kernel(start_ref, first_ref, other, *rest):
    *outs, pieces, buf, sems, acc, across = rest
    copies = fetches([other], buf, sems, pairs_of(start_ref.shape[0], other.shape[1]))
    count = first_ref.shape[0]
    pieces[:count] = first_ref[...]
    overlap(start_ref, pieces.at[count:], buf, acc, across, copies)
    spread(pieces, outs)


def next_kernel(act, nx, *refs):
    prev_ref, kron_ref, start_ref, inv_ref, buf, state_ref, share_ref, *rest = refs[nx:]
    *outs, pieces, acc, across = rest
    set_updated(state_ref, refs[:nx], prev_ref, kron_ref, start_ref, inv_ref, act)
    set_share(state_ref, share_ref, act)
    overlap(state_ref, pieces, buf, acc, across)
    spread(pieces, outs)


def last_kernel(act, nx, *refs):
    prev_ref, kron_ref, start_ref, inv_ref, state_ref = refs[nx:]
    set_updated(state_ref, refs[:nx], prev_ref, kron_ref, start_ref, inv_ref, act)


def kron_kernel(fock_ref, out_ref):
    act = fock_ref.shape[1]
    block = GROUP * act
    row = lax.broadcasted_iota(jnp.int32, (block, act), 0)
    col = lax.broadcasted_iota(jnp.int32, (block, act), 1)
    pick = jnp.where(lax.rem(row, act) == col, 1.0, 0.0).astype(BF16)
    row = lax.broadcasted_iota(jnp.int32, (block, block), 0)
    col = lax.broadcasted_iota(jnp.int32, (block, block), 1)
    same = lax.div(row, act) == lax.div(col, act)
    last = ((1,), (1,))
    for part in range(2):
        value = fock_ref[part]
        head = value.astype(BF16)
        rest = (value - head.astype(F32)).astype(BF16)
        tables = []
        for term in (head, rest):
            table = mxu(mxu(pick, term, last).astype(BF16), pick, last)
            tables.append(jnp.where(same, table, 0.0))
        out_ref[part * block : (part + 1) * block, :] = jnp.concatenate(
            [tables[0], tables[0], tables[1]], axis=1
        ).astype(BF16)


def output_kernel(act, mine_ref, theirs_ref, out_ref):
    core = lax.axis_index("c")
    avir = out_ref.shape[1]
    low = mine_ref.shape[0] // act
    at = lane((low, LANES))

    @pl.loop(0, act // 2, unroll=3)
    def _(pair):
        order = []
        for k in range(2):
            where = pl.ds(2 * pair + k, low, stride=act)
            mine, theirs = mine_ref[where, :], theirs_ref[where, :]
            order.append(jnp.where(core == 0, mine, theirs))
            order.append(jnp.where(core == 0, theirs, mine))
        for side in range(2):
            for part in range(2):
                value = None
                for n in (3, 2, 1, 0):
                    shift = (32 * n - 64 * side - 32 * part) % LANES
                    moved = pltpu.roll(order[n], shift, 1) if shift else order[n]
                    value = moved if value is None else jnp.where(at < 32 * (n + 1), moved, value)
                rows = low if side == 0 else avir - low
                where = pl.ds(pl.multiple_of(pair * LANES, LANES), LANES)
                out_ref[part, pl.ds(side * low, rows), where] = value[:rows]


def total_of(refs, at, rows):
    total = refs[0][at : at + rows, :].astype(F32)
    for ref in refs[1:]:
        total += ref[at : at + rows, :].astype(F32)
    return total


def along_z_kernel(*refs):
    *recvs, share_ref, out_ref = refs
    nz, rows, _ = out_ref.shape
    depth = rows - share_ref.shape[0]
    share = share_ref[...]
    for z in range(nz):
        out_ref[z, :depth, :] = total_of(recvs, z * depth, depth).astype(BF16)
        out_ref[z, depth:, :] = share


def sum_kernel(recv_ref, out_ref):
    nz, rows, _ = out_ref.shape
    total = total_of([recv_ref.at[z] for z in range(nz)], 0, rows).astype(BF16)
    for i in range(nz):
        out_ref[i] = total


def couple_kernel(recv_ref, couple_ref, out_ref):
    nz, height, _ = recv_ref.shape
    ny, rows, _ = out_ref.shape
    low = couple_ref.shape[1] // (2 * nz)
    base = height - rows
    couple = couple_ref[...]
    half = couple.shape[0] // 2

    @pl.loop(0, rows // (2 * low))
    def _(n):
        at = pl.multiple_of(n * 2 * low, 16)
        lines = []
        for z in range(nz):
            there = pl.ds(pl.multiple_of(base + n * 2 * low, 16), 2 * low)
            both = recv_ref[z, there, :].astype(F32)
            lines += merged(both[:low], both[low:])
        both = mxu(couple, jnp.concatenate(lines, axis=0).astype(BF16))
        term = both[:half] + turned(both[half:])
        for y in range(ny):
            top = y * 2 * low
            pieces = merged(term[top : top + low], term[top + low : top + 2 * low])
            out_ref[y, pl.ds(at, 2 * low), :] = jnp.concatenate(pieces, axis=0).astype(BF16)


def along_y_kernel(inter_ref, vir_ref, *outs):
    nz, depth, _ = inter_ref.shape
    me = lax.axis_index("y")
    for k, out in enumerate(outs):
        for z in range(nz):
            out[z * depth : (z + 1) * depth, :] = inter_ref[z]
        out[nz * depth :, :] = vir_ref[me ^ k]


def tail_kernel(act, height, *refs):
    *recvs, buf, out_ref, inter_ref, both, total, right, recv_sems = refs
    rows = out_ref.shape[0]
    nfit = buf.shape[3]
    me = lax.axis_index("y")
    moves = [
        pltpu.make_async_copy(recv, inter_ref.at[me ^ k], recv_sems.at[k])
        for k, recv in enumerate(recvs)
    ]
    for move in moves:
        move.start()
    for move in moves:
        move.wait()
    wide = inter_ref.shape[0] * height // LANES
    tiles = {}
    for slot in range(0, 16 * wide, 2):
        piece, at = divmod(slot * 8, height)
        pair = inter_ref[piece, at : at + 16, :].astype(F32)
        tiles[slot], tiles[slot + 1] = pair[:8], pair[8:]
    count = -(-nfit // LANES)
    lines = [
        jnp.concatenate([tiles[g * wide + k] for k in range(count)], axis=1)
        for g in range(16)
    ]
    for s in range(2):
        re = jnp.concatenate(lines[8 * s : 8 * s + 4], axis=0)
        im = jnp.concatenate(lines[8 * s + 4 : 8 * s + 8], axis=0)
        for k, order in enumerate(((re, im), (-im, re))):
            right[s, k] = jnp.concatenate([*order, *order], axis=0).astype(BF16)

    depth = 2 * rows // STRIPS

    @pl.loop(0, STRIPS)
    def _(n):
        there = pl.ds(pl.multiple_of(n * depth, 16), depth)
        here = None
        for s in range(2):
            for k in range(2):
                term = mxu(buf[s, k, there, :], right[s, k], ((1,), (1,)))
                here = term if here is None else here + term
        both[there, :] = here

    first_half = lane((rows, LANES)) < 64
    total[...] = jnp.where(first_half, both[:rows, :], both[rows:, :])
    low = rows // act
    share = (inter_ref.shape[1] - height) // low
    held = [inter_ref.at[y] for y in range(inter_ref.shape[0])]
    first = lax.axis_index("x") * share
    for i in range(0, share, 2):
        pair = total_of(held, height + i * low, 2 * low)
        for k in range(2):
            where = pl.ds(first + i + k, low, stride=act)
            total[where, :] = total[where, :] + pair[k * low : (k + 1) * low]
    out_ref[...] = total[...].astype(BF16)


VMEM = pl.BlockSpec(memory_space=pltpu.VMEM)
ANY = pl.BlockSpec(memory_space=pl.ANY)
HBM = pl.BlockSpec(memory_space=pltpu.HBM)
SMEM = pl.BlockSpec(memory_space=pltpu.SMEM)


def call(body, outs, ins, scratch=(), name=None, flops=0, moved=0, limit=LARGE, out=VMEM):
    return pl.pallas_call(
        body,
        out_shape=outs,
        in_specs=ins,
        out_specs=jax.tree.map(lambda _: out, outs),
        scratch_shapes=scratch,
        compiler_params=pltpu.CompilerParams(vmem_limit_bytes=limit if moved else SMALL),
        cost_estimate=pl.CostEstimate(flops=flops, bytes_accessed=moved, transcendentals=0),
        name=name,
    )


def exchange(copies, axis):
    return lax.all_to_all(copies, axis, 0, 0, tiled=True)


def swapped(values, axis):
    size = len(values)
    return [values[0]] + [
        lax.ppermute(values[k], axis, [(i, i ^ k) for i in range(size)]) for k in range(1, size)
    ]


def laid_out(couple, low, ny):
    nz, _, avir, _ = couple.shape
    couple = couple.reshape(nz, 2, avir, ny, avir)
    fill = (0, 2 * low - avir)
    couple = jnp.pad(couple, ((0, 0), (0, 0), fill, (0, 0), fill))
    return couple.transpose(1, 3, 4, 0, 2).reshape(4 * ny * low, 2 * nz * low)


def per_device(fitted, vcouple, actfock, eps_vir, eps_act, pair_energy, source):
    cores, nx, ny, nz = (lax.axis_size(n) for n in ("c", "x", "y", "z"))
    core = lax.axis_index("c")
    _, avir, act, nfit = fitted.shape
    pairs = pair_energy.shape[0]
    half = pairs // cores
    width = avir * act
    low = low_count(avir)
    rows = low * act
    share = act // nx
    swap = [(0, 1), (1, 0)]
    own = fitted.reshape(2, width, nfit)
    other = lax.ppermute(own, "c", swap)

    mine = lax.dynamic_slice_in_dim(vcouple, lax.axis_index("y") * avir, avir, 1)
    mine = lax.dynamic_slice_in_dim(mine, lax.axis_index("z") * avir * ny, avir * ny, 2)
    couple = exchange(jnp.broadcast_to(mine[None], (nz, *mine.shape)), FIT)

    energy = lax.dynamic_slice_in_dim(pair_energy, core * half, half, 0)
    energy = jnp.tile(energy, LANES // half).reshape(1, LANES)

    wide = tiles_per_row(nfit, ny * nz)
    height = 16 * wide * 8 // ny
    depth = height // nz
    extra = share * low

    def sent(*shape):
        return jax.ShapeDtypeStruct((*shape, LANES), BF16)

    state_shape = jax.ShapeDtypeStruct((rows, LANES), F32)
    piece_shape, share_shape = [sent(height)] * ny, sent(extra)
    pieces = pltpu.VMEM((ny, height, LANES), BF16)
    steps = steps_of(rows)

    def fetch(count):
        return [
            pltpu.VMEM((count, 2, buffer_rows(rows), nfit), BF16),
            pltpu.SemaphoreType.DMA((max(steps, STRIPS), count, 2)),
        ]

    def sums(count):
        return fetch(count) + [
            pltpu.VMEM((count, 64, nfit), F32), pltpu.VMEM((2, 2, 64, steps * CHUNK), BF16)
        ]

    flops = 16 * width * nfit * 32
    moved = 8 * width * nfit
    opening = call(
        functools.partial(opening_kernel, act),
        [state_shape, state_shape, share_shape, sent(ny // 2, height)],
        [VMEM, VMEM, SMEM, VMEM, HBM], sums(1), "opening", flops // 2, moved // 2,
    )
    second = call(
        second_kernel, piece_shape, [VMEM, VMEM, HBM], [pieces] + sums(1), "second",
        flops // 2, moved // 2,
    )
    later = call(
        functools.partial(next_kernel, act, nx), [state_shape, share_shape] + piece_shape,
        [VMEM] * (nx + 5), [pieces] + sums(2)[2:], "later", flops, moved // 4, MIDDLE,
    )
    stage = call(
        stage_kernel, jax.ShapeDtypeStruct((2, 2, buffer_rows(rows), nfit), BF16),
        [ANY, HBM, HBM],
        [
            pltpu.VMEM((2, buffer_rows(rows) - width, nfit), BF16),
            pltpu.SemaphoreType.DMA((2, 2)),
        ],
        "stage", 0, 4 * moved, 4 << 20, ANY,
    )
    last = call(
        functools.partial(last_kernel, act, nx), state_shape, [VMEM] * (nx + 4), (), "last"
    )
    block = GROUP * act
    kron = call(
        kron_kernel, jax.ShapeDtypeStruct((2 * block, 3 * block), BF16), [VMEM], (), "kron"
    )(actfock)
    along_z = call(
        along_z_kernel, sent(nz, depth + extra), [VMEM] * (ny + 1), (), "along_z"
    )
    summed = call(sum_kernel, sent(nz, depth), [VMEM], (), "summed")
    coupled = call(couple_kernel, sent(ny, extra), [VMEM] * 2, (), "coupled")
    along_y = call(
        along_y_kernel, [sent(height + extra)] * ny, [VMEM] * 2, (), "along_y"
    )
    tail = call(
        functools.partial(tail_kernel, act, height), sent(rows),
        [HBM] * ny + [VMEM],
        [
            pltpu.VMEM((ny, height + extra, LANES), BF16),
            pltpu.VMEM((2 * rows, LANES), F32),
            pltpu.VMEM((rows, LANES), F32),
            pltpu.VMEM((2, 2, LANES, nfit), BF16),
            pltpu.SemaphoreType.DMA((ny,)),
        ],
        "tail", flops, moved // 4, MIDDLE,
    )
    output = call(
        functools.partial(output_kernel, act),
        jax.ShapeDtypeStruct((2, avir, act * pairs), F32), [VMEM] * 2, (), "output",
    )

    for step in range(PASSES):
        if step == 0:
            start, inverse, share_now, part = opening(
                source, eps_vir.reshape(avir, 1), eps_act, energy, own
            )
            state = start
            part = second(start, part, other)
            part, couple = lax.optimization_barrier((part, couple))
            couple = laid_out(couple, low, ny)
        else:
            state, share_now, *part = later(*recv, state, kron, start, inverse, blocks)
        mixed = exchange(along_z(*swapped(part, "y"), share_now), "z")
        inter = exchange(summed(mixed), "z")
        mixed = along_y(inter, coupled(mixed, couple))
        blocks = stage(mixed[0], own, other)
        recv = swapped([tail(*swapped(mixed, "y"), blocks)] * nx, "x")
    state = last(*recv, state, kron, start, inverse)
    return output(state, lax.ppermute(state, "c", swap))


def solution(mesh, sizes=(8, 4, 4, 2)):
    in_specs = (
        P(None, VIR, None, FIT),
        P(None, FIT, None),
        P(),
        P(VIR),
        P(),
        P(),
        P(None, VIR, None),
    )
    return jax.shard_map(
        per_device,
        mesh=Mesh(mesh.devices.reshape(*sizes), ("z", "y", "x", "c")),
        in_specs=in_specs,
        out_specs=P(None, VIR, None),
        check_vma=False,
    )
```

```python
import functools

import jax
import jax.numpy as jnp
from jax import lax
from jax.experimental import pallas as pl
from jax.experimental.pallas import tpu as pltpu
from jax.sharding import Mesh
from jax.sharding import PartitionSpec as P

PASSES = 3
VIR = ("z", "y")
FIT = ("x", "c")
F32 = jnp.float32
BF16 = jnp.bfloat16
LANES = 128
GROUP = 10
CHUNK = 256
STRIPS = 4
LARGE = 36 << 20
MIDDLE = 20 << 20
SMALL = 12 << 20


def low_count(avir):
    return -(-avir // (2 * GROUP)) * GROUP


def lane(shape):
    return lax.broadcasted_iota(jnp.int32, shape, len(shape) - 1)


def turned(both):
    ahead = pltpu.roll(both, LANES - 32, 1)
    behind = pltpu.roll(both, 32, 1)
    return jnp.where((lane(both.shape) & 32) == 0, -ahead, behind)


def merged(left, right):
    first = lane(left.shape) < 64
    return (
        jnp.where(first, left, pltpu.roll(right, 64, 1)),
        jnp.where(first, pltpu.roll(left, 64, 1), right),
    )


def mxu(left, right, dims=((1,), (0,))):
    return lax.dot_general(left, right, (dims, ((), ())), preferred_element_type=F32)


def steps_of(rows):
    return -(-rows // CHUNK)


def buffer_rows(rows):
    return rows + steps_of(rows) * CHUNK


def pairs_of(rows, width):
    out = []
    for at in range(0, rows, CHUNK):
        ends = ((at, min(at + CHUNK, rows)), (rows + at, min(rows + at + CHUNK, width)))
        out.append([(first, end) for first, end in ends if end > first])
    return out


def fetches(blocks, buf, sems, plan):
    width = blocks[0].shape[1]
    buf[:, :, width:, :] = jnp.zeros(
        (buf.shape[0], 2, buf.shape[2] - width, buf.shape[3]), BF16
    )
    copies = []
    for n, ranges in enumerate(plan):
        step = []
        for s, ref in enumerate(blocks):
            for k, (first, end) in enumerate(ranges):
                where = pl.ds(first, end - first)
                step.append(
                    pltpu.make_async_copy(
                        ref.at[:, where, :], buf.at[s, :, where, :], sems.at[n, s, k]
                    )
                )
        copies.append(step)
    for step in copies:
        for copy in step:
            copy.start()
    return copies


def wait_for(copies, n):
    for i, step in enumerate(copies):

        @pl.when(n == i)
        def _():
            for copy in step:
                copy.wait()


def tiles_per_row(nfit, vir_count):
    count = -(-nfit // LANES)
    while 16 * count % (2 * vir_count):
        count += 1
    return count


def set_updated(state_ref, recvs, prev_ref, kron_ref, start_ref, inv_ref, act):
    block = GROUP * act

    @pl.loop(0, start_ref.shape[0] // block, unroll=2 if start_ref.shape[0] % (2 * block) == 0 else 1)
    def _(n):
        where = pl.ds(pl.multiple_of(n * block, block), block)
        value = prev_ref[where, :]
        head = value.astype(BF16)
        tail = (value - head.astype(F32)).astype(BF16)
        both = mxu(kron_ref[...], jnp.concatenate([head, tail, head], axis=0))
        values = [recv[where, :].astype(F32) for recv in recvs]
        while len(values) > 1:
            values = [values[i] + values[i + 1] for i in range(0, len(values), 2)]
        total = both[:block] + turned(both[block:]) + values[0]
        state_ref[where, :] = start_ref[where, :] - total * inv_ref[where, :]


def set_share(state_ref, share_ref, act):
    low = state_ref.shape[0] // act
    count = share_ref.shape[0] // low
    first = lax.axis_index("x") * count
    for i in range(0, count, 2):
        both = [state_ref[pl.ds(first + i + k, low, stride=act), :] for k in range(2)]
        share_ref[i * low : (i + 2) * low, :] = jnp.concatenate(both, axis=0).astype(BF16)


def overlap(state_ref, pieces_ref, buf, acc, across, copies=()):
    rows = state_ref.shape[0]
    value = state_ref[...].T
    spare = jnp.zeros((64, across.shape[3] - rows), F32)
    for half in range(2):
        re = value[64 * half : 64 * half + 32]
        im = value[64 * half + 32 : 64 * half + 64]
        for k, order in enumerate(((re, im), (im, -re))):
            both = jnp.concatenate([jnp.concatenate(order, axis=0), spare], axis=1)
            across[half, k] = both.astype(BF16)
    count = buf.shape[0]
    acc[...] = jnp.zeros(acc.shape, F32)

    @pl.loop(0, steps_of(rows))
    def _(n):
        wait_for(copies, n)
        here = pl.ds(pl.multiple_of(n * CHUNK, CHUNK), CHUNK)
        left = [[across[half, k, :, here] for k in range(2)] for half in range(2)]
        for s in range(count):
            total = None
            for half in range(2):
                there = pl.ds(pl.multiple_of(half * rows + n * CHUNK, 16), CHUNK)
                for k in range(2):
                    term = mxu(left[half][k], buf[s, k, there, :])
                    total = term if total is None else total + term
            acc[s] += total

    sums = [acc[s] for s in range(count)]
    nfit = sums[0].shape[1]
    pieces, depth, _ = pieces_ref.shape
    groups = 8 * count
    wide = pieces * depth // (8 * groups)

    def tile(slot):
        group, k = divmod(slot, wide)
        if k * LANES >= nfit:
            return jnp.zeros((8, LANES), F32)
        s, at = divmod(group * 8, 64)
        return sums[s][at : at + 8, k * LANES : (k + 1) * LANES]

    for slot in range(0, groups * wide, 2):
        both = jnp.concatenate([tile(slot), tile(slot + 1)], axis=0).astype(BF16)
        piece, at = divmod(slot * 8, depth)
        pieces_ref[piece, at : at + 16, :] = both


def spread(pieces_ref, outs):
    me = lax.axis_index("y")
    for k, out in enumerate(outs):
        out[...] = pieces_ref[me ^ k]


def prepare(source_ref, vir_ref, act_ref, pair_ref, start_ref, inv_ref, act):
    core = lax.axis_index("c")
    avir = source_ref.shape[0]
    low = start_ref.shape[0] // act
    spare = 2 * low - avir
    at = lane((low, LANES))
    row = lax.broadcasted_iota(jnp.int32, (low, LANES), 0)
    held = (at < 64) | (row < low - spare)

    def lifted(values, fill):
        rest = jnp.full((spare, values.shape[1]), fill, F32)
        return values[:low], jnp.concatenate([values[low:], rest], axis=0)

    above = lifted(jnp.broadcast_to(vir_ref[...], (avir, LANES)), 1.0)
    above = jnp.where(at < 64, above[0], above[1]) - pair_ref[...]

    @pl.loop(0, act // 2, unroll=3)
    def _(pair):
        sides = []
        for part in range(2):
            where = pl.ds(pl.multiple_of(pair * LANES, LANES), LANES)
            values = source_ref[:, part, where]
            values = jnp.where(core == 0, values, pltpu.roll(values, LANES - 32, 1))
            sides += lifted(values, 0.0)
        order = (sides[0], sides[2], sides[1], sides[3])
        for k in range(2):
            t = 2 * pair + k
            value = None
            for n in (3, 2, 1, 0):
                shift = (32 * n - 64 * k) % LANES
                moved = pltpu.roll(order[n], shift, 1) if shift else order[n]
                value = moved if value is None else jnp.where(at < 32 * (n + 1), moved, value)
            inverse = jnp.where(held, 1.0 / (above + act_ref[t]), 0.0)
            inv_ref[pl.ds(t, low, stride=act), :] = inverse
            start_ref[pl.ds(t, low, stride=act), :] = value * inverse


def stage_kernel(after, own, other, buf, zeros, sems):
    width = own.shape[1]
    zeros[...] = jnp.zeros(zeros.shape, BF16)
    copies = []
    for s, ref in enumerate((own, other)):
        copies.append(pltpu.make_async_copy(ref, buf.at[s, :, pl.ds(0, width), :], sems.at[s, 0]))
        there = buf.at[s, :, pl.ds(width, zeros.shape[1]), :]
        copies.append(pltpu.make_async_copy(zeros, there, sems.at[s, 1]))
    for copy in copies:
        copy.start()
    for copy in copies:
        copy.wait()


def opening_kernel(
    act, source_ref, vir_ref, act_ref, pair_ref, own,
    start_ref, inv_ref, share_ref, pieces_ref, *scratch,
):
    buf, sems, acc, across = scratch
    copies = fetches([own], buf, sems, pairs_of(start_ref.shape[0], own.shape[1]))
    prepare(source_ref, vir_ref, act_ref, pair_ref, start_ref, inv_ref, act)
    set_share(start_ref, share_ref, act)
    overlap(start_ref, pieces_ref, buf, acc, across, copies)


def second_kernel(start_ref, first_ref, other, *rest):
    *outs, pieces, buf, sems, acc, across = rest
    copies = fetches([other], buf, sems, pairs_of(start_ref.shape[0], other.shape[1]))
    count = first_ref.shape[0]
    pieces[:count] = first_ref[...]
    overlap(start_ref, pieces.at[count:], buf, acc, across, copies)
    spread(pieces, outs)


def next_kernel(act, nx, *refs):
    prev_ref, kron_ref, start_ref, inv_ref, buf, state_ref, share_ref, *rest = refs[nx:]
    *outs, pieces, acc, across = rest
    set_updated(state_ref, refs[:nx], prev_ref, kron_ref, start_ref, inv_ref, act)
    set_share(state_ref, share_ref, act)
    overlap(state_ref, pieces, buf, acc, across)
    spread(pieces, outs)


def last_kernel(act, nx, *refs):
    prev_ref, kron_ref, start_ref, inv_ref, state_ref = refs[nx:]
    set_updated(state_ref, refs[:nx], prev_ref, kron_ref, start_ref, inv_ref, act)


def kron_kernel(fock_ref, out_ref):
    act = fock_ref.shape[1]
    block = GROUP * act
    row = lax.broadcasted_iota(jnp.int32, (block, act), 0)
    col = lax.broadcasted_iota(jnp.int32, (block, act), 1)
    pick = jnp.where(lax.rem(row, act) == col, 1.0, 0.0).astype(BF16)
    row = lax.broadcasted_iota(jnp.int32, (block, block), 0)
    col = lax.broadcasted_iota(jnp.int32, (block, block), 1)
    same = lax.div(row, act) == lax.div(col, act)
    last = ((1,), (1,))
    for part in range(2):
        value = fock_ref[part]
        head = value.astype(BF16)
        rest = (value - head.astype(F32)).astype(BF16)
        tables = []
        for term in (head, rest):
            table = mxu(mxu(pick, term, last).astype(BF16), pick, last)
            tables.append(jnp.where(same, table, 0.0))
        out_ref[part * block : (part + 1) * block, :] = jnp.concatenate(
            [tables[0], tables[0], tables[1]], axis=1
        ).astype(BF16)


def output_kernel(act, mine_ref, theirs_ref, out_ref):
    core = lax.axis_index("c")
    avir = out_ref.shape[0]
    low = mine_ref.shape[0] // act
    at = lane((low, LANES))

    @pl.loop(0, act // 2, unroll=3)
    def _(pair):
        order = []
        for k in range(2):
            where = pl.ds(2 * pair + k, low, stride=act)
            mine, theirs = mine_ref[where, :], theirs_ref[where, :]
            order.append(jnp.where(core == 0, mine, theirs))
            order.append(jnp.where(core == 0, theirs, mine))
        for side in range(2):
            for part in range(2):
                value = None
                for n in (3, 2, 1, 0):
                    shift = (32 * n - 64 * side - 32 * part) % LANES
                    moved = pltpu.roll(order[n], shift, 1) if shift else order[n]
                    value = moved if value is None else jnp.where(at < 32 * (n + 1), moved, value)
                rows = low if side == 0 else avir - low
                where = pl.ds(pl.multiple_of(pair * LANES, LANES), LANES)
                out_ref[pl.ds(side * low, rows), part, where] = value[:rows]


def total_of(refs, at, rows):
    total = refs[0][at : at + rows, :].astype(F32)
    for ref in refs[1:]:
        total += ref[at : at + rows, :].astype(F32)
    return total


def along_z_kernel(*refs):
    *recvs, share_ref, out_ref = refs
    nz, rows, _ = out_ref.shape
    depth = rows - share_ref.shape[0]
    share = share_ref[...]
    for z in range(nz):
        out_ref[z, :depth, :] = total_of(recvs, z * depth, depth).astype(BF16)
        out_ref[z, depth:, :] = share


def sum_kernel(recv_ref, out_ref):
    nz, rows, _ = out_ref.shape
    total = total_of([recv_ref.at[z] for z in range(nz)], 0, rows).astype(BF16)
    for i in range(nz):
        out_ref[i] = total


def couple_kernel(recv_ref, couple_ref, out_ref):
    nz, height, _ = recv_ref.shape
    ny, rows, _ = out_ref.shape
    low = couple_ref.shape[1] // (2 * nz)
    base = height - rows
    couple = couple_ref[...]
    half = couple.shape[0] // 2

    @pl.loop(0, rows // (2 * low))
    def _(n):
        at = pl.multiple_of(n * 2 * low, 16)
        lines = []
        for z in range(nz):
            there = pl.ds(pl.multiple_of(base + n * 2 * low, 16), 2 * low)
            both = recv_ref[z, there, :].astype(F32)
            lines += merged(both[:low], both[low:])
        both = mxu(couple, jnp.concatenate(lines, axis=0).astype(BF16))
        term = both[:half] + turned(both[half:])
        for y in range(ny):
            top = y * 2 * low
            pieces = merged(term[top : top + low], term[top + low : top + 2 * low])
            out_ref[y, pl.ds(at, 2 * low), :] = jnp.concatenate(pieces, axis=0).astype(BF16)


def along_y_kernel(inter_ref, vir_ref, *outs):
    nz, depth, _ = inter_ref.shape
    me = lax.axis_index("y")
    for k, out in enumerate(outs):
        for z in range(nz):
            out[z * depth : (z + 1) * depth, :] = inter_ref[z]
        out[nz * depth :, :] = vir_ref[me ^ k]


def tail_kernel(act, height, *refs):
    *recvs, buf, out_ref, inter_ref, both, total, right, recv_sems = refs
    rows = out_ref.shape[0]
    nfit = buf.shape[3]
    me = lax.axis_index("y")
    moves = [
        pltpu.make_async_copy(recv, inter_ref.at[me ^ k], recv_sems.at[k])
        for k, recv in enumerate(recvs)
    ]
    for move in moves:
        move.start()
    for move in moves:
        move.wait()
    wide = inter_ref.shape[0] * height // LANES
    tiles = {}
    for slot in range(0, 16 * wide, 2):
        piece, at = divmod(slot * 8, height)
        pair = inter_ref[piece, at : at + 16, :].astype(F32)
        tiles[slot], tiles[slot + 1] = pair[:8], pair[8:]
    count = -(-nfit // LANES)
    lines = [
        jnp.concatenate([tiles[g * wide + k] for k in range(count)], axis=1)
        for g in range(16)
    ]
    for s in range(2):
        re = jnp.concatenate(lines[8 * s : 8 * s + 4], axis=0)
        im = jnp.concatenate(lines[8 * s + 4 : 8 * s + 8], axis=0)
        for k, order in enumerate(((re, im), (-im, re))):
            right[s, k] = jnp.concatenate([*order, *order], axis=0).astype(BF16)

    depth = 2 * rows // STRIPS

    @pl.loop(0, STRIPS)
    def _(n):
        there = pl.ds(pl.multiple_of(n * depth, 16), depth)
        here = None
        for s in range(2):
            for k in range(2):
                term = mxu(buf[s, k, there, :], right[s, k], ((1,), (1,)))
                here = term if here is None else here + term
        both[there, :] = here

    first_half = lane((rows, LANES)) < 64
    total[...] = jnp.where(first_half, both[:rows, :], both[rows:, :])
    low = rows // act
    share = (inter_ref.shape[1] - height) // low
    held = [inter_ref.at[y] for y in range(inter_ref.shape[0])]
    first = lax.axis_index("x") * share
    for i in range(0, share, 2):
        pair = total_of(held, height + i * low, 2 * low)
        for k in range(2):
            where = pl.ds(first + i + k, low, stride=act)
            total[where, :] = total[where, :] + pair[k * low : (k + 1) * low]
    out_ref[...] = total[...].astype(BF16)


VMEM = pl.BlockSpec(memory_space=pltpu.VMEM)
ANY = pl.BlockSpec(memory_space=pl.ANY)
HBM = pl.BlockSpec(memory_space=pltpu.HBM)
SMEM = pl.BlockSpec(memory_space=pltpu.SMEM)


def call(body, outs, ins, scratch=(), name=None, flops=0, moved=0, limit=LARGE, out=VMEM):
    return pl.pallas_call(
        body,
        out_shape=outs,
        in_specs=ins,
        out_specs=jax.tree.map(lambda _: out, outs),
        scratch_shapes=scratch,
        compiler_params=pltpu.CompilerParams(vmem_limit_bytes=limit if moved else SMALL),
        cost_estimate=pl.CostEstimate(flops=flops, bytes_accessed=moved, transcendentals=0),
        name=name,
    )


def exchange(copies, axis):
    return lax.all_to_all(copies, axis, 0, 0, tiled=True)


def swapped(values, axis):
    size = len(values)
    return [values[0]] + [
        lax.ppermute(values[k], axis, [(i, i ^ k) for i in range(size)]) for k in range(1, size)
    ]


def laid_out(couple, low, ny):
    nz, _, avir, _ = couple.shape
    couple = couple.reshape(nz, 2, avir, ny, avir)
    fill = (0, 2 * low - avir)
    couple = jnp.pad(couple, ((0, 0), (0, 0), fill, (0, 0), fill))
    return couple.transpose(1, 3, 4, 0, 2).reshape(4 * ny * low, 2 * nz * low)


def per_device(fitted, vcouple, actfock, eps_vir, eps_act, pair_energy, source):
    cores, nx, ny, nz = (lax.axis_size(n) for n in ("c", "x", "y", "z"))
    core = lax.axis_index("c")
    _, avir, act, nfit = fitted.shape
    pairs = pair_energy.shape[0]
    half = pairs // cores
    width = avir * act
    low = low_count(avir)
    rows = low * act
    share = act // nx
    swap = [(0, 1), (1, 0)]
    own = fitted.reshape(2, width, nfit)
    other = lax.ppermute(own, "c", swap)

    mine = lax.dynamic_slice_in_dim(vcouple, lax.axis_index("y") * avir, avir, 1)
    mine = lax.dynamic_slice_in_dim(mine, lax.axis_index("z") * avir * ny, avir * ny, 2)
    couple = exchange(jnp.broadcast_to(mine[None], (nz, *mine.shape)), FIT)

    energy = lax.dynamic_slice_in_dim(pair_energy, core * half, half, 0)
    energy = jnp.tile(energy, LANES // half).reshape(1, LANES)

    wide = tiles_per_row(nfit, ny * nz)
    height = 16 * wide * 8 // ny
    depth = height // nz
    extra = share * low

    def sent(*shape):
        return jax.ShapeDtypeStruct((*shape, LANES), BF16)

    state_shape = jax.ShapeDtypeStruct((rows, LANES), F32)
    piece_shape, share_shape = [sent(height)] * ny, sent(extra)
    pieces = pltpu.VMEM((ny, height, LANES), BF16)
    steps = steps_of(rows)

    def fetch(count):
        return [
            pltpu.VMEM((count, 2, buffer_rows(rows), nfit), BF16),
            pltpu.SemaphoreType.DMA((max(steps, STRIPS), count, 2)),
        ]

    def sums(count):
        return fetch(count) + [
            pltpu.VMEM((count, 64, nfit), F32), pltpu.VMEM((2, 2, 64, steps * CHUNK), BF16)
        ]

    flops = 16 * width * nfit * 32
    moved = 8 * width * nfit
    opening = call(
        functools.partial(opening_kernel, act),
        [state_shape, state_shape, share_shape, sent(ny // 2, height)],
        [VMEM, VMEM, SMEM, VMEM, HBM], sums(1), "opening", flops // 2, moved // 2,
    )
    second = call(
        second_kernel, piece_shape, [VMEM, VMEM, HBM], [pieces] + sums(1), "second",
        flops // 2, moved // 2,
    )
    later = call(
        functools.partial(next_kernel, act, nx), [state_shape, share_shape] + piece_shape,
        [VMEM] * (nx + 5), [pieces] + sums(2)[2:], "later", flops, moved // 4, MIDDLE,
    )
    stage = call(
        stage_kernel, jax.ShapeDtypeStruct((2, 2, buffer_rows(rows), nfit), BF16),
        [ANY, HBM, HBM],
        [
            pltpu.VMEM((2, buffer_rows(rows) - width, nfit), BF16),
            pltpu.SemaphoreType.DMA((2, 2)),
        ],
        "stage", 0, 4 * moved, 4 << 20, ANY,
    )
    last = call(
        functools.partial(last_kernel, act, nx), state_shape, [VMEM] * (nx + 4), (), "last"
    )
    block = GROUP * act
    kron = call(
        kron_kernel, jax.ShapeDtypeStruct((2 * block, 3 * block), BF16), [VMEM], (), "kron"
    )(actfock)
    along_z = call(
        along_z_kernel, sent(nz, depth + extra), [VMEM] * (ny + 1), (), "along_z"
    )
    summed = call(sum_kernel, sent(nz, depth), [VMEM], (), "summed")
    coupled = call(couple_kernel, sent(ny, extra), [VMEM] * 2, (), "coupled")
    along_y = call(
        along_y_kernel, [sent(height + extra)] * ny, [VMEM] * 2, (), "along_y"
    )
    tail = call(
        functools.partial(tail_kernel, act, height), sent(rows),
        [HBM] * ny + [VMEM],
        [
            pltpu.VMEM((ny, height + extra, LANES), BF16),
            pltpu.VMEM((2 * rows, LANES), F32),
            pltpu.VMEM((rows, LANES), F32),
            pltpu.VMEM((2, 2, LANES, nfit), BF16),
            pltpu.SemaphoreType.DMA((ny,)),
        ],
        "tail", flops, moved // 4, MIDDLE,
    )
    output = call(
        functools.partial(output_kernel, act),
        jax.ShapeDtypeStruct((avir, 2, act * pairs), F32), [VMEM] * 2, (), "output",
    )

    for step in range(PASSES):
        if step == 0:
            start, inverse, share_now, part = opening(
                source.transpose(1, 0, 2), eps_vir.reshape(avir, 1), eps_act, energy, own
            )
            state = start
            part = second(start, part, other)
        else:
            state, share_now, *part = later(*recv, state, kron, start, inverse, blocks)
        mixed = along_z(*swapped(part, "y"), share_now)
        if step == 0:
            mixed, couple = lax.optimization_barrier((mixed, couple))
            couple = laid_out(couple, low, ny)
        mixed = exchange(mixed, "z")
        inter = exchange(summed(mixed), "z")
        mixed = along_y(inter, coupled(mixed, couple))
        blocks = stage(mixed[0], own, other)
        recv = swapped([tail(*swapped(mixed, "y"), blocks)] * nx, "x")
    state = last(*recv, state, kron, start, inverse)
    return output(state, lax.ppermute(state, "c", swap)).transpose(1, 0, 2)


def solution(mesh, sizes=(8, 4, 4, 2)):
    in_specs = (
        P(None, VIR, None, FIT),
        P(None, FIT, None),
        P(),
        P(VIR),
        P(),
        P(),
        P(None, VIR, None),
    )
    return jax.shard_map(
        per_device,
        mesh=Mesh(mesh.devices.reshape(*sizes), ("z", "y", "x", "c")),
        in_specs=in_specs,
        out_specs=P(None, VIR, None),
        check_vma=False,
    )
```
